256 devices in a mesh: prow: 16 (over z, core), pcol: 16 (over x, y).
Axes of the slice: x: 4, y: 4, z: 8, core: 2. Of those that a mesh axis runs over, the one named last changes fastest.
Arguments:
- right_side: float32 [7, 4096, 256], P(None, 'prow'), may hold values from -6 to 6
- inverse_diag: float32 [7, 4096, 4096], P(None, 'pcol', 'prow'), as said below
- panels: float32 [7, 16384, 4096], P(None, 'prow', 'pcol'), may hold values from -0.09375 to 0.09375
- block_rows: int32 [7, 128], P(None, 'prow'), may hold values from 128 to 479, as said below
Outputs:
- solution: float32 [7, 4096, 256], P(None, 'pcol')
- upper_update: float32 [32768, 256], P(('prow', 'pcol'))
The draws below stay inside these ranges and needn't reach their ends.
Inputs may be any that keep to these rules, and one draw needn't show every extreme that they name: inverse_diag[k] is lower triangular with a positive diagonal. block_rows[k, j] is a block row of an ancestor of supernode k or an upper block row, and the entries of one supernode are distinct. The entries j with j // 8 = p lie in blocks p * 2 to (p + 1) * 2 - 1 of an ancestor's rows or in upper block rows p * 16 to (p + 1) * 16 - 1.
All inputs are finite; a program needn't handle non-finite values.
Results may differ from the reference program's by a relative error of at most 0.00011.
Values sent between devices are 32-bit elements; how exact they have to be, the bound alone decides.
A program may use at most 64 MiB of HBM per device.

```python
import jax
import jax.numpy as jnp
import numpy as np
from jax import lax

BLOCK_ROWS = 128
SUPER_BLOCKS = 32
SUPERNODES = 7
RHS_COLS = 256
SLOTS_DEV = 8
ORDER = 4096
PANEL_BLOCKS = 128
UPPER_BLOCKS = 256
OWN_BLOCKS = 2


def shuffle_row(row_key, values):
    return jax.random.permutation(row_key, values)


def draw_block_rows(key, part):
    proc_rows = SUPER_BLOCKS // OWN_BLOCKS
    windowed = SUPERNODES * SUPER_BLOCKS
    upper_own = UPPER_BLOCKS // proc_rows
    rows_out = []
    for node in range(SUPERNODES):
        if node < 4:
            ancestors = [4 + node // 2, 6]
        elif node < 6:
            ancestors = [6]
        else:
            ancestors = []
        listing = []
        for proc_row in range(proc_rows):
            entries = []
            for ancestor in ancestors:
                entries += [ancestor * SUPER_BLOCKS + proc_row * OWN_BLOCKS + offset for offset in range(OWN_BLOCKS)]
            entries += [windowed + proc_row * upper_own + offset for offset in range(upper_own)]
            listing.append(entries)
        index_table = np.array(listing, np.int32)
        if node < SUPERNODES - 1:
            anchor = jnp.asarray(index_table[:, :1])
            others = jnp.asarray(index_table[:, 1:])
        else:
            anchor = jnp.asarray(index_table[:, -1:])
            others = jnp.asarray(index_table[:, :-1])
        row_keys = jax.random.split(jax.random.fold_in(key, node + 11), proc_rows)
        shuffled = jax.vmap(shuffle_row)(row_keys, others)
        chosen = jnp.concatenate([anchor, shuffled[:, :SLOTS_DEV - 1]], axis=1)
        rows_out.append(chosen.reshape(-1))
    return jnp.stack(rows_out).astype(jnp.int32)


def draw_inverse_diag(key, part):
    key_one, key_two = jax.random.split(jax.random.fold_in(key, 5))
    spread = jax.random.normal(key_one, (SUPERNODES, ORDER, ORDER), jnp.float32)
    diagonal_values = jnp.exp(jax.random.uniform(key_two, (SUPERNODES, ORDER, 1), jnp.float32, -0.69, 0.69))
    row_ids = jax.lax.broadcasted_iota(jnp.int32, (1, ORDER, ORDER), 1)
    col_ids = jax.lax.broadcasted_iota(jnp.int32, (1, ORDER, ORDER), 2)
    lower = jnp.where(col_ids < row_ids, spread * (0.6 / float(ORDER) ** 0.5), 0.0)
    return (lower + jnp.where(col_ids == row_ids, diagonal_values, 0.0)).astype(jnp.float32)


def steps_of(own_key, extent, cuts, low, largest):
    loudness, own = 1.0, jax.random.fold_in(own_key, 6)
    for position, blocks in cuts:
        draws = jnp.exp(jax.random.uniform(jax.random.fold_in(own, position), (blocks,), jnp.float32, low / len(cuts), largest / len(cuts)))
        loudness = loudness * jnp.repeat(draws, extent[position] // blocks).reshape([-1 if axis == position else 1 for axis in range(len(extent))])
    return loudness


def noise(rng, shape, scale, most, cuts=(), kind=jnp.bfloat16):
    values = jax.random.normal(rng, shape, jnp.float32) * scale
    if len(cuts) > 0:
        values = steps_of(rng, shape, cuts, -0.22, 0.18) * values
    return jnp.clip(values, min=-most, max=most).astype(kind)


def setup_inputs(seed: int = 0) -> dict:
    key_of = jax.random.split(jax.random.key(seed), 5)
    return {
        "right_side": noise(key_of[0], (SUPERNODES, ORDER, RHS_COLS), 1.0, 6.0, ((1, 16),), jnp.float32),
        "inverse_diag": draw_inverse_diag(jax.random.fold_in(key_of[4], 71), 0),
        "panels": noise(key_of[2], (SUPERNODES, PANEL_BLOCKS * BLOCK_ROWS, ORDER), ORDER ** -0.5, 0.09375, ((1, 16), (2, 16)), jnp.float32),
        "block_rows": draw_block_rows(jax.random.fold_in(key_of[4], 71), 0),
    }


def reference(right_side, inverse_diag, panels, block_rows):
    windowed = SUPERNODES * SUPER_BLOCKS
    updates = jnp.zeros((windowed + UPPER_BLOCKS, BLOCK_ROWS, RHS_COLS), jnp.float32)
    solved = []
    for node in range(SUPERNODES):
        start = node * SUPER_BLOCKS
        own_sums = updates[start:start + SUPER_BLOCKS].reshape(ORDER, RHS_COLS)
        residual = right_side[node] - own_sums
        solution = jnp.dot(inverse_diag[node], residual, precision=lax.Precision.HIGHEST)
        solved.append(solution)
        products = jnp.dot(panels[node], solution, precision=lax.Precision.HIGHEST)
        products = products.reshape(PANEL_BLOCKS, BLOCK_ROWS, RHS_COLS)
        updates = updates.at[block_rows[node]].add(products)
    upper_update = updates[windowed:].reshape(UPPER_BLOCKS * BLOCK_ROWS, RHS_COLS)
    return jnp.stack(solved), upper_update
```

```python
import functools

import jax
import jax.numpy as jnp
from jax import lax
from jax.experimental import pallas as pl
from jax.experimental.pallas import tpu as pltpu
from jax.sharding import PartitionSpec as P

BLOCK_ROWS = 128
SUPER_BLOCKS = 32
SUPERNODES = 7
LEVELS = ((0, 4), (4, 2), (6, 1))
MESH = pl.DeviceIdType.MESH
F32 = jnp.float32
BF16 = jnp.bfloat16


def split(value):
    high = value.astype(BF16)
    low = (value - high.astype(F32)).astype(BF16)
    return high, low


def dot3(a_high, a_low, b_high, b_low):
    dot = functools.partial(jnp.dot, preferred_element_type=F32)
    return dot(a_high, b_high) + (dot(a_high, b_low) + dot(a_low, b_high))


def wait_bytes(ref, sem):
    pltpu.make_async_copy(ref, ref, sem).wait()


def kernel(
    chips, cols, inv_ref, rhs_hbm, diag_hbm, panel_hbm, sol_hbm, up_hbm,
    rhs, diag, panel, panel_high, panel_low, terms, pair_in, half, ring_in, xs, prod,
    win0, win1, win_in0, win_in1, res, piece0, piece1, upper, upper_in, up_out,
    load_sem, panel_sem, pair_send, pair_recv, ring_send, ring_recv, gather_send, gather_recv,
    share_send, share_recv, win_send, win_recv, back_send, back_recv, up_send, up_recv, out_sem,
):
    prow = lax.axis_index("prow")
    pcol = lax.axis_index("pcol")
    chip, core = prow // 2, prow % 2
    other = chip * 2 + 1 - core
    own_half, other_half = core * BLOCK_ROWS, (1 - core) * BLOCK_ROWS
    rows = BLOCK_ROWS // chips
    own_rows = own_half + chip * rows

    loads = []
    for level, (first, count) in enumerate(LEVELS):
        nodes = pl.ds(first, count)
        loads.append((
            pltpu.make_async_copy(rhs_hbm.at[nodes], rhs.at[nodes], load_sem.at[2 * level]),
            pltpu.make_async_copy(diag_hbm.at[nodes], diag.at[nodes], load_sem.at[2 * level + 1]),
        ))
    for pair in loads:
        for copy in pair:
            copy.start()
    panel_loads = [
        pltpu.make_async_copy(panel_hbm.at[k], panel.at[k], panel_sem.at[k]) for k in range(SUPERNODES)
    ]
    for copy in panel_loads:
        copy.start()

    barrier = pltpu.get_barrier_semaphore()
    pl.semaphore_signal(barrier, inc=1, device_id=(other, pcol), device_id_type=MESH)

    def greet_chip(i, carry):
        peer = lax.rem(chip + i, chips) * 2 + core
        pl.semaphore_signal(barrier, inc=1, device_id=(peer, pcol), device_id_type=MESH)
        return carry

    def greet_col(i, carry):
        pl.semaphore_signal(
            barrier, inc=1, device_id=(prow, lax.rem(pcol + i, cols)), device_id_type=MESH
        )
        return carry

    lax.fori_loop(1, chips, greet_chip, 0)
    lax.fori_loop(1, cols, greet_col, 0)
    pl.semaphore_wait(barrier, chips + cols - 1)

    def solve_terms(node, residual):
        d_high, d_low = split(diag[node])
        r_high, r_low = split(residual)
        terms[node] = dot3(d_high, d_low, r_high, r_low)
        pltpu.make_async_remote_copy(
            src_ref=terms.at[node, pl.ds(other_half, BLOCK_ROWS)], dst_ref=pair_in.at[node],
            send_sem=pair_send.at[node], recv_sem=pair_recv.at[node],
            device_id=(other, pcol), device_id_type=MESH,
        ).start()

    def scatter_half(node, carry):
        wait_bytes(pair_in.at[node], pair_recv.at[node])
        half[node] = terms[node, pl.ds(own_half, BLOCK_ROWS)] + pair_in[node]

        def send(i, inner):
            peer = lax.rem(chip + i, chips)
            pltpu.make_async_remote_copy(
                src_ref=half.at[node, pl.ds(peer * rows, rows)], dst_ref=ring_in.at[node, i],
                send_sem=ring_send.at[node], recv_sem=ring_recv.at[node],
                device_id=(peer * 2 + core, pcol), device_id_type=MESH,
            ).start()
            return inner

        lax.fori_loop(1, chips, send, 0)
        return carry

    def gather_half(node, carry):
        wait_bytes(ring_in.at[node, pl.ds(1, chips - 1)], ring_recv.at[node])
        total = half[node, pl.ds(chip * rows, rows)]
        for i in range(1, chips):
            total = total + ring_in[node, i]
        xs[node, pl.ds(own_rows, rows)] = total

        def send(i, inner):
            peer = lax.rem(chip + i, chips)
            pltpu.make_async_remote_copy(
                src_ref=xs.at[node, pl.ds(own_rows, rows)], dst_ref=xs.at[node, pl.ds(own_rows, rows)],
                send_sem=gather_send.at[node], recv_sem=gather_recv.at[node],
                device_id=(peer * 2 + core, pcol), device_id_type=MESH,
            ).start()
            return inner

        lax.fori_loop(1, chips, send, 0)
        return carry

    def share_half(node, carry):
        wait_bytes(ring_in.at[node, pl.ds(1, chips - 1)], gather_recv.at[node])
        pltpu.make_async_remote_copy(
            src_ref=xs.at[node, pl.ds(own_half, BLOCK_ROWS)],
            dst_ref=xs.at[node, pl.ds(own_half, BLOCK_ROWS)],
            send_sem=share_send.at[node], recv_sem=share_recv.at[node],
            device_id=(other, pcol), device_id_type=MESH,
        ).start()
        return carry

    def multiply(node, carry):
        wait_bytes(xs.at[node, pl.ds(other_half, BLOCK_ROWS)], share_recv.at[node])
        x_high, x_low = split(xs[node])

        def quarter(b, inner):
            part = pl.ds(b * 256, 256)
            product = dot3(panel_high[node, part], panel_low[node, part], x_high, x_low)
            prod[node, 2 * b] = product[:BLOCK_ROWS]
            prod[node, 2 * b + 1] = product[BLOCK_ROWS:]
            return inner

        lax.fori_loop(0, 4, quarter, 0)
        return carry

    def split_panels(first, count):
        for node in range(first, first + count):
            panel_loads[node].wait()

        def one(step, carry):
            node, part = first + step // 8, pl.ds((step % 8) * BLOCK_ROWS, BLOCK_ROWS)
            high, low = split(panel[node, part])
            panel_high[node, part] = high
            panel_low[node, part] = low
            return carry

        lax.fori_loop(0, 8 * count, one, 0)

    def solve_level(level, residual_of, between):
        first, count = LEVELS[level]
        for copy in loads[level]:
            copy.wait()

        def begin(node, carry):
            solve_terms(node, residual_of(node))
            return carry

        lax.fori_loop(first, first + count, begin, 0)
        lax.fori_loop(first, first + count, scatter_half, 0)
        between()
        lax.fori_loop(first, first + count, gather_half, 0)
        lax.fori_loop(first, first + count, share_half, 0)
        lax.fori_loop(first, first + count, multiply, 0)

    def picked(node, dest):
        return prod[node, inv_ref[node, dest]]

    def add_upper(first, count, fresh):
        def one(j, carry):
            total = picked(first, 6 + j)
            for node in range(first + 1, first + count):
                total = total + picked(node, 6 + j)
            upper[j] = total if fresh else upper[j] + total
            return carry

        lax.fori_loop(0, upper.shape[0], one, 0)

    def reduce_window(which, win, win_in, piece, first):
        size = win.shape[0] // cols

        def send(i, carry):
            peer = lax.rem(pcol + i, cols)
            pltpu.make_async_remote_copy(
                src_ref=win.at[pl.ds(peer * size, size)], dst_ref=win_in.at[i],
                send_sem=win_send.at[which], recv_sem=win_recv.at[which],
                device_id=(prow, peer), device_id_type=MESH,
            ).start()
            return carry

        lax.fori_loop(1, cols, send, 0)

        def finish():
            wait_bytes(win_in.at[pl.ds(1, cols - 1)], win_recv.at[which])
            total = win[pl.ds(pcol * size, size)]
            for i in range(1, cols):
                total = total + win_in[i]
            begin = first * 2 * BLOCK_ROWS + pcol * size
            node, row = begin // (2 * BLOCK_ROWS), begin % (2 * BLOCK_ROWS)
            here = res.at[node - 4, pl.ds(row, size)]
            res[node - 4, pl.ds(row, size)] = rhs[node, pl.ds(row, size)] - total

            def spread(i, carry):
                pltpu.make_async_remote_copy(
                    src_ref=here, dst_ref=here,
                    send_sem=back_send.at[which], recv_sem=back_recv.at[which],
                    device_id=(prow, lax.rem(pcol + i, cols)), device_id_type=MESH,
                ).start()
                return carry

            lax.fori_loop(1, cols, spread, 0)
            wait_bytes(win_in.at[pl.ds(1, cols - 1)], back_recv.at[which])

        return finish

    def store_solution(level):
        first, count = LEVELS[level]
        nodes = pl.ds(first, count)
        copy = pltpu.make_async_copy(xs.at[nodes], sol_hbm.at[nodes], out_sem.at[level])
        copy.start()
        return copy

    def prepare():
        def clear(node, carry):
            prod[node, 8] = jnp.zeros((BLOCK_ROWS, prod.shape[3]), F32)
            return carry

        lax.fori_loop(0, SUPERNODES, clear, 0)
        split_panels(0, 4)

    solve_level(0, lambda node: rhs[node], prepare)
    stores = [store_solution(0)]
    for j in range(4):
        child = 2 * (j // 2)
        win0[pl.ds(j * BLOCK_ROWS, BLOCK_ROWS)] = picked(child, j) + picked(child + 1, j)
    finish = reduce_window(0, win0, win_in0, piece0, 4)
    add_upper(0, 4, True)
    for copy in loads[1]:
        copy.wait()
    loads[1] = ()
    finish()

    solve_level(1, lambda node: res[node - 4], lambda: split_panels(4, 2))
    stores.append(store_solution(1))
    for j in range(2):
        total = picked(0, 4 + j)
        for node in range(1, 6):
            total = total + picked(node, 4 + j)
        win1[pl.ds(j * BLOCK_ROWS, BLOCK_ROWS)] = total
    finish = reduce_window(1, win1, win_in1, piece1, 6)
    add_upper(4, 2, False)
    for copy in loads[2]:
        copy.wait()
    loads[2] = ()
    finish()

    solve_level(2, lambda node: res[node - 4], lambda: split_panels(6, 1))
    stores.append(store_solution(2))
    add_upper(6, 1, False)
    size = upper.shape[0] // cols

    def send_upper(i, carry):
        peer = lax.rem(pcol + i, cols)
        pltpu.make_async_remote_copy(
            src_ref=upper.at[pl.ds(peer * size, size)], dst_ref=upper_in.at[i],
            send_sem=up_send, recv_sem=up_recv, device_id=(prow, peer), device_id_type=MESH,
        ).start()
        return carry

    lax.fori_loop(1, cols, send_upper, 0)
    wait_bytes(upper_in.at[pl.ds(1, cols - 1)], up_recv)

    for b in range(size):
        def sum_rows(t, carry):
            part = pl.ds(t * 32, 32)
            total = upper[pcol * size + b, part]
            for i in range(1, cols):
                total = total + upper_in[i, b, part]
            up_out[b, part] = total
            return carry

        lax.fori_loop(0, BLOCK_ROWS // 32, sum_rows, 0)
    last = pltpu.make_async_copy(up_out, up_hbm, out_sem.at[3])
    last.start()

    def drain(node, carry):
        wait_bytes(pair_in.at[node], pair_send.at[node])
        wait_bytes(ring_in.at[node, pl.ds(1, chips - 1)], ring_send.at[node])
        wait_bytes(ring_in.at[node, pl.ds(1, chips - 1)], gather_send.at[node])
        wait_bytes(pair_in.at[node], share_send.at[node])
        return carry

    lax.fori_loop(0, SUPERNODES, drain, 0)
    for which, win_in in enumerate((win_in0, win_in1)):
        wait_bytes(win_in.at[pl.ds(1, cols - 1)], win_send.at[which])
        wait_bytes(win_in.at[pl.ds(1, cols - 1)], back_send.at[which])
    wait_bytes(upper_in.at[pl.ds(1, cols - 1)], up_send)
    for copy in stores:
        copy.wait()
    last.wait()


def inverse_map(block_rows, own_blocks, upper_own, super_blocks):
    proc_row = lax.axis_index("prow")
    windowed = SUPERNODES * super_blocks
    node_of = block_rows // super_blocks
    local_win = (node_of - 4) * own_blocks + block_rows % super_blocks - proc_row * own_blocks
    local_up = 3 * own_blocks + block_rows - windowed - proc_row * upper_own
    local = jnp.where(block_rows < windowed, local_win, local_up)
    slots = block_rows.shape[1]
    dest = lax.broadcasted_iota(jnp.int32, (1, 3 * own_blocks + upper_own, 1), 1)
    slot = lax.broadcasted_iota(jnp.int32, (1, 1, slots), 2)
    return jnp.min(jnp.where(dest == local[:, None, :], slot, slots), axis=2)


def per_device(chips, cols, super_blocks, right_side, inverse_diag, panels, block_rows):
    rhs_cols = right_side.shape[2]
    order = right_side.shape[1]
    own_blocks = order // BLOCK_ROWS
    upper_own = 2 * block_rows.shape[1]
    inverse = inverse_map(block_rows, own_blocks, upper_own, super_blocks)
    rows = BLOCK_ROWS // chips
    win_rows = (4 * BLOCK_ROWS, 2 * BLOCK_ROWS)
    size = upper_own // cols
    dma = pltpu.SemaphoreType.DMA
    scratch = [
        pltpu.VMEM((7, order, rhs_cols), F32),
        pltpu.VMEM((7, order, order), F32),
        pltpu.VMEM(panels.shape, F32),
        pltpu.VMEM(panels.shape, BF16),
        pltpu.VMEM(panels.shape, BF16),
        pltpu.VMEM((7, order, rhs_cols), F32),
        pltpu.VMEM((7, BLOCK_ROWS, rhs_cols), F32),
        pltpu.VMEM((7, BLOCK_ROWS, rhs_cols), F32),
        pltpu.VMEM((7, chips, rows, rhs_cols), F32),
        pltpu.VMEM((7, order, rhs_cols), F32),
        pltpu.VMEM((7, 9, BLOCK_ROWS, rhs_cols), F32),
        pltpu.VMEM((win_rows[0], rhs_cols), F32),
        pltpu.VMEM((win_rows[1], rhs_cols), F32),
        pltpu.VMEM((cols, win_rows[0] // cols, rhs_cols), F32),
        pltpu.VMEM((cols, win_rows[1] // cols, rhs_cols), F32),
        pltpu.VMEM((3, order, rhs_cols), F32),
        pltpu.VMEM((8, rhs_cols), F32),
        pltpu.VMEM((8, rhs_cols), F32),
        pltpu.VMEM((upper_own, BLOCK_ROWS, rhs_cols), F32),
        pltpu.VMEM((cols, size, BLOCK_ROWS, rhs_cols), F32),
        pltpu.VMEM((size, BLOCK_ROWS, rhs_cols), F32),
        dma((6,)), dma((7,)),
        dma((7,)), dma((7,)), dma((7,)), dma((7,)), dma((7,)), dma((7,)),
        dma((7,)), dma((7,)), dma((2,)), dma((2,)), dma((2,)), dma((2,)),
        dma, dma, dma((4,)),
    ]
    anywhere = pl.BlockSpec(memory_space=pl.ANY)
    solved, upper = pl.pallas_call(
        functools.partial(kernel, chips, cols),
        out_shape=(
            jax.ShapeDtypeStruct((7, order, rhs_cols), F32),
            jax.ShapeDtypeStruct((size, BLOCK_ROWS, rhs_cols), F32),
        ),
        in_specs=[pl.BlockSpec(memory_space=pltpu.SMEM), anywhere, anywhere, anywhere],
        out_specs=(anywhere, anywhere),
        scratch_shapes=scratch,
        compiler_params=pltpu.CompilerParams(
            collective_id=0, has_side_effects=True, vmem_limit_bytes=56 * 1024 * 1024
        ),
    )(inverse, right_side, inverse_diag, panels)
    return solved, upper.reshape(size * BLOCK_ROWS, rhs_cols)


def solution(mesh):
    chips, cols = mesh.shape["prow"] // 2, mesh.shape["pcol"]
    super_blocks = 2 * mesh.shape["prow"]
    in_specs = (
        P(None, "prow", None),
        P(None, "pcol", "prow"),
        P(None, "prow", "pcol"),
        P(None, "prow"),
    )
    out_specs = (P(None, "pcol", None), P(("prow", "pcol"), None))
    return jax.shard_map(
        functools.partial(per_device, chips, cols, super_blocks),
        mesh=mesh, in_specs=in_specs, out_specs=out_specs, check_vma=False,
    )
```

```python
import functools
import math

import jax
import jax.numpy as jnp
from jax import lax
from jax.experimental import pallas as pl
from jax.experimental.pallas import tpu as pltpu
from jax.sharding import PartitionSpec as P

BLOCK_ROWS = 128
SUPER_BLOCKS = 32
SUPERNODES = 7
MESH = pl.DeviceIdType.MESH
F32 = jnp.float32
BF16 = jnp.bfloat16


def split(value):
    high = value.astype(BF16)
    low = (value - high.astype(F32)).astype(BF16)
    return high, low


def dot3(a_high, a_low, b_high, b_low):
    dot = functools.partial(jnp.dot, preferred_element_type=F32)
    return dot(a_high, b_high) + (dot(a_high, b_low) + dot(a_low, b_high))


def wait_bytes(ref, sem):
    pltpu.make_async_copy(ref, ref, sem).wait()


def kernel(
    chips, side, inv_ref, rhs_hbm, diag_hbm, panel_hbm, sol_hbm, up_hbm,
    rhs, diag, panel, panel_high, panel_low, terms, pair_in, half, ring_in, xs, prod,
    win, win_in, res, upper, up_in, up_mid, up_last, up_out,
    rhs_sem, diag_sem, panel_sem, pair_send, pair_recv, ring_send, ring_recv,
    gather_send, gather_recv, share_send, share_recv, win_send, win_recv, back_send, back_recv,
    up_send, up_recv, last_send, last_recv, out_sem,
):
    cols = side * side
    prow = lax.axis_index("prow")
    pcol = lax.axis_index("pcol")
    chip, core = prow // 2, prow % 2
    col_x, col_y = pcol // side, pcol % side
    other = chip * 2 + 1 - core
    own_half, other_half = core * BLOCK_ROWS, (1 - core) * BLOCK_ROWS
    rows = BLOCK_ROWS // chips
    own_rows = own_half + chip * rows
    sent = []

    loads = {}
    for k in range(SUPERNODES):
        loads["rhs", k] = pltpu.make_async_copy(rhs_hbm.at[k], rhs.at[k], rhs_sem.at[k])
        loads["diag", k] = pltpu.make_async_copy(diag_hbm.at[k], diag.at[k], diag_sem.at[k])
        loads["panel", k] = pltpu.make_async_copy(panel_hbm.at[k], panel.at[k], panel_sem.at[k])
    for k in range(4):
        loads["rhs", k].start()
        loads["diag", k].start()
    for k in range(SUPERNODES):
        if k >= 4:
            loads["rhs", k].start()
            loads["diag", k].start()
        loads["panel", k].start()

    barrier = pltpu.get_barrier_semaphore()
    pl.semaphore_signal(barrier, inc=1, device_id=(other, pcol), device_id_type=MESH)

    def greet_chip(i, carry):
        peer = lax.rem(chip + i, chips) * 2 + core
        pl.semaphore_signal(barrier, inc=1, device_id=(peer, pcol), device_id_type=MESH)
        return carry

    def greet_col(i, carry):
        pl.semaphore_signal(
            barrier, inc=1, device_id=(prow, lax.rem(pcol + i, cols)), device_id_type=MESH
        )
        return carry

    lax.fori_loop(1, chips, greet_chip, 0)
    lax.fori_loop(1, cols, greet_col, 0)

    def begin_node(node, residual):
        d_high, d_low = split(diag[node])
        r_high, r_low = split(residual[...])
        terms[node] = dot3(d_high, d_low, r_high, r_low)

    def pair_node(node):
        pltpu.make_async_remote_copy(
            src_ref=terms.at[node, pl.ds(other_half, BLOCK_ROWS)], dst_ref=pair_in.at[node],
            send_sem=pair_send.at[node], recv_sem=pair_recv.at[node],
            device_id=(other, pcol), device_id_type=MESH,
        ).start()
        sent.append((pair_in.at[node], pair_send.at[node]))

    def scatter_node(node):
        wait_bytes(pair_in.at[node], pair_recv.at[node])
        half[node] = terms[node, pl.ds(own_half, BLOCK_ROWS)] + pair_in[node]

        def send(i, inner):
            peer = lax.rem(chip + i, chips)
            pltpu.make_async_remote_copy(
                src_ref=half.at[node, pl.ds(peer * rows, rows)], dst_ref=ring_in.at[node, i],
                send_sem=ring_send.at[node], recv_sem=ring_recv.at[node],
                device_id=(peer * 2 + core, pcol), device_id_type=MESH,
            ).start()
            return inner

        lax.fori_loop(1, chips, send, 0)
        sent.append((ring_in.at[node, pl.ds(1, chips - 1)], ring_send.at[node]))

    def gather_node(node):
        wait_bytes(ring_in.at[node, pl.ds(1, chips - 1)], ring_recv.at[node])
        total = half[node, pl.ds(chip * rows, rows)]
        for i in range(1, chips):
            total = total + ring_in[node, i]
        xs[node, pl.ds(own_rows, rows)] = total
        here = xs.at[node, pl.ds(own_rows, rows)]

        def send(i, inner):
            peer = lax.rem(chip + i, chips)
            pltpu.make_async_remote_copy(
                src_ref=here, dst_ref=here,
                send_sem=gather_send.at[node], recv_sem=gather_recv.at[node],
                device_id=(peer * 2 + core, pcol), device_id_type=MESH,
            ).start()
            return inner

        lax.fori_loop(1, chips, send, 0)
        sent.append((ring_in.at[node, pl.ds(1, chips - 1)], gather_send.at[node]))

    def share_node(node):
        wait_bytes(ring_in.at[node, pl.ds(1, chips - 1)], gather_recv.at[node])
        here = xs.at[node, pl.ds(own_half, BLOCK_ROWS)]
        pltpu.make_async_remote_copy(
            src_ref=here, dst_ref=here,
            send_sem=share_send.at[node], recv_sem=share_recv.at[node],
            device_id=(other, pcol), device_id_type=MESH,
        ).start()
        sent.append((pair_in.at[node], share_send.at[node]))

    def multiply_node(node):
        wait_bytes(xs.at[node, pl.ds(other_half, BLOCK_ROWS)], share_recv.at[node])
        x_high, x_low = split(xs[node])

        def quarter(b, inner):
            part = pl.ds(b * 256, 256)
            product = dot3(panel_high[node, part], panel_low[node, part], x_high, x_low)
            prod[node, 2 * b] = product[:BLOCK_ROWS]
            prod[node, 2 * b + 1] = product[BLOCK_ROWS:]
            return inner

        lax.fori_loop(0, 4, quarter, 0)

    def store_node(node):
        copy = pltpu.make_async_copy(xs.at[node], sol_hbm.at[node], out_sem.at[node])
        copy.start()
        return copy

    def split_panel(node):
        loads["panel", node].wait()

        def one(step, carry):
            part = pl.ds(step * BLOCK_ROWS, BLOCK_ROWS)
            panel_high[node, part], panel_low[node, part] = split(panel[node, part])
            return carry

        lax.fori_loop(0, 8, one, 0)

    def picked(node, dest):
        return prod[node, inv_ref[node, dest]]

    size = 2 * BLOCK_ROWS // cols

    def send_window(target, nodes):
        which = target - 4
        for b in range(2):
            total = picked(nodes[0], 2 * which + b)
            for node in nodes[1:]:
                total = total + picked(node, 2 * which + b)
            win[which, pl.ds(b * BLOCK_ROWS, BLOCK_ROWS)] = total

        def send(i, carry):
            peer = lax.rem(pcol + i, cols)
            pltpu.make_async_remote_copy(
                src_ref=win.at[which, pl.ds(peer * size, size)], dst_ref=win_in.at[which, i],
                send_sem=win_send.at[which], recv_sem=win_recv.at[which],
                device_id=(prow, peer), device_id_type=MESH,
            ).start()
            return carry

        lax.fori_loop(1, cols, send, 0)
        sent.append((win_in.at[which, pl.ds(1, cols - 1)], win_send.at[which]))

    def spread_window(target):
        which = target - 4
        loads["rhs", target].wait()
        wait_bytes(win_in.at[which, pl.ds(1, cols - 1)], win_recv.at[which])
        mine = pl.ds(pcol * size, size)
        total = win[which, mine]
        for i in range(1, cols):
            total = total + win_in[which, i]
        res[which, mine] = rhs[target, mine] - total
        here = res.at[which, mine]

        def spread(i, carry):
            pltpu.make_async_remote_copy(
                src_ref=here, dst_ref=here,
                send_sem=back_send.at[which], recv_sem=back_recv.at[which],
                device_id=(prow, lax.rem(pcol + i, cols)), device_id_type=MESH,
            ).start()
            return carry

        lax.fori_loop(1, cols, spread, 0)
        sent.append((win_in.at[which, pl.ds(1, cols - 1)], back_send.at[which]))

    def begin_parent(target):
        which = target - 4
        loads["diag", target].wait()
        wait_bytes(win_in.at[which, pl.ds(1, cols - 1)], back_recv.at[which])
        begin_node(target, res.at[which])
        pair_node(target)

    def add_upper(which, nodes, fresh):
        count = upper.shape[3] // BLOCK_ROWS

        def one(j, carry):
            total = picked(nodes[0], 6 + j)
            for node in nodes[1:]:
                total = total + picked(node, 6 + j)
            place = j // count
            part = pl.ds((j % count) * BLOCK_ROWS, BLOCK_ROWS)
            spot = (which, place // side, place % side, part)
            upper[spot] = total if fresh else upper[spot] + total
            return carry

        lax.fori_loop(0, cols * count, one, 0)

    up_rows = upper.shape[3] // 2
    first_rows, second_rows = pl.ds(0, up_rows), pl.ds(up_rows, up_rows)

    def send_upper(which):
        for i in range(1, side):
            peer_x, peer_y = lax.rem(col_x + i, side), lax.rem(col_y + i, side)
            pltpu.make_async_remote_copy(
                src_ref=upper.at[which, peer_x, :, first_rows], dst_ref=up_in.at[which, 0, i],
                send_sem=up_send.at[which, 0], recv_sem=up_recv.at[which, 0],
                device_id=(prow, peer_x * side + col_y), device_id_type=MESH,
            ).start()
            pltpu.make_async_remote_copy(
                src_ref=upper.at[which, :, peer_y, second_rows], dst_ref=up_in.at[which, 1, i],
                send_sem=up_send.at[which, 1], recv_sem=up_recv.at[which, 1],
                device_id=(prow, col_x * side + peer_y), device_id_type=MESH,
            ).start()
        for way in range(2):
            sent.append((up_in.at[which, way, pl.ds(1, side - 1)], up_send.at[which, way]))

    def middle_upper(which):
        for way in range(2):
            wait_bytes(up_in.at[which, way, pl.ds(1, side - 1)], up_recv.at[which, way])

            def one(j, carry):
                if way == 0:
                    total = upper[which, col_x, j, first_rows]
                else:
                    total = upper[which, j, col_y, second_rows]
                for i in range(1, side):
                    total = total + up_in[which, way, i, j]
                up_mid[which, way, j] = total
                return carry

            lax.fori_loop(0, side, one, 0)
            for i in range(1, side):
                if way == 0:
                    place = lax.rem(col_y + i, side)
                    peer = col_x * side + place
                else:
                    place = lax.rem(col_x + i, side)
                    peer = place * side + col_y
                pltpu.make_async_remote_copy(
                    src_ref=up_mid.at[which, way, place], dst_ref=up_last.at[which, way, i],
                    send_sem=last_send.at[which, way], recv_sem=last_recv.at[which, way],
                    device_id=(prow, peer), device_id_type=MESH,
                ).start()
            sent.append((up_last.at[which, way, pl.ds(1, side - 1)], last_send.at[which, way]))

    def finish_upper(which, fresh):
        for way in range(2):
            wait_bytes(up_last.at[which, way, pl.ds(1, side - 1)], last_recv.at[which, way])
            total = up_mid[which, way, col_y if way == 0 else col_x]
            for i in range(1, side):
                total = total + up_last[which, way, i]
            part = first_rows if way == 0 else second_rows
            up_out[part] = total if fresh else up_out[part] + total

    def run():
        for node in range(4):
            loads["rhs", node].wait()
            loads["diag", node].wait()
            begin_node(node, rhs.at[node])
            if node == 0:
                pl.semaphore_wait(barrier, chips + cols - 1)
            pair_node(node)
        yield
        for node in range(4):
            scatter_node(node)
        for node in range(SUPERNODES):
            prod[node, 8] = jnp.zeros((BLOCK_ROWS, prod.shape[3]), F32)
        for node in range(2):
            split_panel(node)
        yield
        for node in range(4):
            gather_node(node)
        for node in range(2, 4):
            split_panel(node)
        yield
        for parent in (4, 5):
            children = (2 * parent - 8, 2 * parent - 7)
            for node in children:
                share_node(node)
            for node in children:
                multiply_node(node)
            send_window(parent, children)
            yield
        for node in range(4, 7):
            split_panel(node)
        spread_window(4)
        spread_window(5)
        yield
        stores = [store_node(node) for node in range(4)]
        add_upper(0, (0, 1, 2, 3), True)
        begin_parent(4)
        begin_parent(5)
        yield
        scatter_node(4)
        scatter_node(5)
        gather_node(4)
        gather_node(5)
        yield
        share_node(4)
        share_node(5)
        multiply_node(4)
        multiply_node(5)
        send_window(6, (0, 1, 2, 3, 4, 5))
        yield
        stores += [store_node(node) for node in (4, 5)]
        add_upper(0, (4, 5), False)
        spread_window(6)
        send_upper(0)
        yield
        begin_parent(6)
        scatter_node(6)
        gather_node(6)
        yield
        middle_upper(0)
        share_node(6)
        multiply_node(6)
        yield
        add_upper(1, (6,), True)
        send_upper(1)
        stores.append(store_node(6))
        finish_upper(0, True)
        middle_upper(1)
        yield
        finish_upper(1, False)
        last = pltpu.make_async_copy(up_out, up_hbm, out_sem.at[7])
        last.start()
        for copy in stores:
            copy.wait()
        last.wait()

    for _ in run():
        pass
    for ref, sem in sent:
        wait_bytes(ref, sem)


def inverse_map(block_rows, own_blocks, upper_own, super_blocks):
    proc_row = lax.axis_index("prow")
    windowed = SUPERNODES * super_blocks
    node_of = block_rows // super_blocks
    local_win = (node_of - 4) * own_blocks + block_rows % super_blocks - proc_row * own_blocks
    local_up = 3 * own_blocks + block_rows - windowed - proc_row * upper_own
    local = jnp.where(block_rows < windowed, local_win, local_up)
    slots = block_rows.shape[1]
    dest = lax.broadcasted_iota(jnp.int32, (1, 3 * own_blocks + upper_own, 1), 1)
    slot = lax.broadcasted_iota(jnp.int32, (1, 1, slots), 2)
    return jnp.min(jnp.where(dest == local[:, None, :], slot, slots), axis=2)


def per_device(chips, side, super_blocks, right_side, inverse_diag, panels, block_rows):
    rhs_cols = right_side.shape[2]
    order = right_side.shape[1]
    own_blocks = order // BLOCK_ROWS
    upper_own = 2 * block_rows.shape[1]
    inverse = inverse_map(block_rows, own_blocks, upper_own, super_blocks)
    rows = BLOCK_ROWS // chips
    cols = side * side
    own_upper = upper_own * BLOCK_ROWS // cols
    dma = pltpu.SemaphoreType.DMA
    scratch = [
        pltpu.VMEM((7, order, rhs_cols), F32),
        pltpu.VMEM((7, order, order), F32),
        pltpu.VMEM(panels.shape, F32),
        pltpu.VMEM(panels.shape, BF16),
        pltpu.VMEM(panels.shape, BF16),
        pltpu.VMEM((7, order, rhs_cols), F32),
        pltpu.VMEM((7, BLOCK_ROWS, rhs_cols), F32),
        pltpu.VMEM((7, BLOCK_ROWS, rhs_cols), F32),
        pltpu.VMEM((7, chips, rows, rhs_cols), F32),
        pltpu.VMEM((7, order, rhs_cols), F32),
        pltpu.VMEM((7, 9, BLOCK_ROWS, rhs_cols), F32),
        pltpu.VMEM((3, order, rhs_cols), F32),
        pltpu.VMEM((3, cols, order // cols, rhs_cols), F32),
        pltpu.VMEM((3, order, rhs_cols), F32),
        pltpu.VMEM((2, side, side, own_upper, rhs_cols), F32),
        pltpu.VMEM((2, 2, side, side, own_upper // 2, rhs_cols), F32),
        pltpu.VMEM((2, 2, side, own_upper // 2, rhs_cols), F32),
        pltpu.VMEM((2, 2, side, own_upper // 2, rhs_cols), F32),
        pltpu.VMEM((own_upper, rhs_cols), F32),
        dma((7,)), dma((7,)), dma((7,)), dma((7,)), dma((7,)), dma((7,)), dma((7,)),
        dma((7,)), dma((7,)), dma((7,)), dma((7,)), dma((3,)), dma((3,)), dma((3,)), dma((3,)),
        dma((2, 2)), dma((2, 2)), dma((2, 2)), dma((2, 2)), dma((8,)),
    ]
    anywhere = pl.BlockSpec(memory_space=pl.ANY)
    return pl.pallas_call(
        functools.partial(kernel, chips, side),
        out_shape=(
            jax.ShapeDtypeStruct((7, order, rhs_cols), F32),
            jax.ShapeDtypeStruct((own_upper, rhs_cols), F32),
        ),
        in_specs=[pl.BlockSpec(memory_space=pltpu.SMEM), anywhere, anywhere, anywhere],
        out_specs=(anywhere, anywhere),
        scratch_shapes=scratch,
        compiler_params=pltpu.CompilerParams(
            collective_id=0, has_side_effects=True, vmem_limit_bytes=58 * 1024 * 1024
        ),
    )(inverse, right_side, inverse_diag, panels)


def solution(mesh):
    chips, side = mesh.shape["prow"] // 2, math.isqrt(mesh.shape["pcol"])
    super_blocks = 2 * mesh.shape["prow"]
    in_specs = (
        P(None, "prow", None),
        P(None, "pcol", "prow"),
        P(None, "prow", "pcol"),
        P(None, "prow"),
    )
    out_specs = (P(None, "pcol", None), P(("prow", "pcol"), None))
    return jax.shard_map(
        functools.partial(per_device, chips, side, super_blocks),
        mesh=mesh, in_specs=in_specs, out_specs=out_specs, check_vma=False,
    )
```

```python
import functools
import math

import jax
import jax.numpy as jnp
from jax import lax
from jax.experimental import pallas as pl
from jax.experimental.pallas import tpu as pltpu
from jax.sharding import PartitionSpec as P

BLOCK_ROWS = 128
SUPER_BLOCKS = 32
SUPERNODES = 7
MESH = pl.DeviceIdType.MESH
F32 = jnp.float32
BF16 = jnp.bfloat16


def split(value):
    high = value.astype(BF16)
    low = (value - high.astype(F32)).astype(BF16)
    return high, low


def dot3(a_high, a_low, b_high, b_low):
    dot = functools.partial(jnp.dot, preferred_element_type=F32)
    return dot(a_high, b_high) + (dot(a_high, b_low) + dot(a_low, b_high))


def wait_bytes(ref, sem):
    pltpu.make_async_copy(ref, ref, sem).wait()


def kernel(
    chips, side, super_blocks, rows_ref, rhs_hbm, diag_hbm, panel_hbm, sol_hbm, up_hbm,
    rhs, diag, panel, panel_high, panel_low, terms, pair_in, half, ring_in, xs, prod,
    win, win_in, res, upper, up_in, up_mid, up_last, up_out,
    rhs_sem, diag_sem, panel_sem, pair_send, pair_recv, ring_send, ring_recv,
    gather_send, gather_recv, share_send, share_recv, win_send, win_recv, back_send, back_recv,
    up_send, up_recv, last_send, last_recv, out_sem,
):
    cols = side * side
    prow = lax.axis_index("prow")
    pcol = lax.axis_index("pcol")
    chip, core = prow // 2, prow % 2
    col_x, col_y = pcol // side, pcol % side
    other = chip * 2 + 1 - core
    own_half, other_half = core * BLOCK_ROWS, (1 - core) * BLOCK_ROWS
    rows = BLOCK_ROWS // chips
    own_rows = own_half + chip * rows
    sent = []

    barrier = pltpu.get_barrier_semaphore()
    pl.semaphore_signal(barrier, inc=1, device_id=(other, pcol), device_id_type=MESH)

    def greet_chip(i, carry):
        peer = lax.rem(chip + i, chips) * 2 + core
        pl.semaphore_signal(barrier, inc=1, device_id=(peer, pcol), device_id_type=MESH)
        return carry

    def greet_col(i, carry):
        pl.semaphore_signal(
            barrier, inc=1, device_id=(prow, lax.rem(pcol + i, cols)), device_id_type=MESH
        )
        return carry

    lax.fori_loop(1, chips, greet_chip, 0)
    lax.fori_loop(1, cols, greet_col, 0)

    loads = {}
    for k in range(SUPERNODES):
        loads["rhs", k] = pltpu.make_async_copy(rhs_hbm.at[k], rhs.at[k], rhs_sem.at[k])
        loads["diag", k] = pltpu.make_async_copy(diag_hbm.at[k], diag.at[k], diag_sem.at[k])
        loads["panel", k] = pltpu.make_async_copy(panel_hbm.at[k], panel.at[k], panel_sem.at[k])
    for k in range(4):
        loads["rhs", k].start()
        loads["diag", k].start()
    for k in range(SUPERNODES):
        if k >= 4:
            loads["rhs", k].start()
            loads["diag", k].start()
        loads["panel", k].start()

    def begin_node(node, residual):
        d_high, d_low = split(diag[node])
        r_high, r_low = split(residual[...])
        terms[node] = dot3(d_high, d_low, r_high, r_low)

    def pair_node(node):
        pltpu.make_async_remote_copy(
            src_ref=terms.at[node, pl.ds(other_half, BLOCK_ROWS)], dst_ref=pair_in.at[node],
            send_sem=pair_send.at[node], recv_sem=pair_recv.at[node],
            device_id=(other, pcol), device_id_type=MESH,
        ).start()
        sent.append((pair_in.at[node], pair_send.at[node]))

    def scatter_node(node):
        wait_bytes(pair_in.at[node], pair_recv.at[node])
        half[node] = terms[node, pl.ds(own_half, BLOCK_ROWS)] + pair_in[node]

        def send(i, inner):
            peer = lax.rem(chip + i, chips)
            pltpu.make_async_remote_copy(
                src_ref=half.at[node, pl.ds(peer * rows, rows)], dst_ref=ring_in.at[node, i],
                send_sem=ring_send.at[node], recv_sem=ring_recv.at[node],
                device_id=(peer * 2 + core, pcol), device_id_type=MESH,
            ).start()
            return inner

        lax.fori_loop(1, chips, send, 0)
        sent.append((ring_in.at[node, pl.ds(1, chips - 1)], ring_send.at[node]))

    def gather_node(node):
        wait_bytes(ring_in.at[node, pl.ds(1, chips - 1)], ring_recv.at[node])
        total = half[node, pl.ds(chip * rows, rows)]
        for i in range(1, chips):
            total = total + ring_in[node, i]
        xs[node, pl.ds(own_rows, rows)] = total
        here = xs.at[node, pl.ds(own_rows, rows)]

        def send(i, inner):
            peer = lax.rem(chip + i, chips)
            pltpu.make_async_remote_copy(
                src_ref=here, dst_ref=here,
                send_sem=gather_send.at[node], recv_sem=gather_recv.at[node],
                device_id=(peer * 2 + core, pcol), device_id_type=MESH,
            ).start()
            return inner

        lax.fori_loop(1, chips, send, 0)
        sent.append((ring_in.at[node, pl.ds(1, chips - 1)], gather_send.at[node]))

    def share_node(node):
        wait_bytes(ring_in.at[node, pl.ds(1, chips - 1)], gather_recv.at[node])
        here = xs.at[node, pl.ds(own_half, BLOCK_ROWS)]
        pltpu.make_async_remote_copy(
            src_ref=here, dst_ref=here,
            send_sem=share_send.at[node], recv_sem=share_recv.at[node],
            device_id=(other, pcol), device_id_type=MESH,
        ).start()
        sent.append((pair_in.at[node], share_send.at[node]))

    def multiply_node(node):
        wait_bytes(xs.at[node, pl.ds(other_half, BLOCK_ROWS)], share_recv.at[node])
        x_high, x_low = split(xs[node])

        product = dot3(panel_high[node], panel_low[node], x_high, x_low)
        for slot in range(8):
            prod[node, slot] = product[slot * BLOCK_ROWS:(slot + 1) * BLOCK_ROWS]

    def store_node(node):
        copy = pltpu.make_async_copy(xs.at[node], sol_hbm.at[node], out_sem.at[node])
        copy.start()
        return copy

    def split_panel(node):
        loads["panel", node].wait()

        def one(step, carry):
            part = pl.ds(step * BLOCK_ROWS, BLOCK_ROWS)
            panel_high[node, part], panel_low[node, part] = split(panel[node, part])
            return carry

        lax.fori_loop(0, 8, one, 0)

    def picked(node, block):
        slot = 8
        for i in range(8):
            slot = jnp.where(rows_ref[node, i] == block, i, slot)
        return prod[node, slot]

    size = 2 * BLOCK_ROWS // cols

    def send_window(target, nodes):
        which = target - 4
        for b in range(2):
            block = target * super_blocks + prow * 2 + b
            total = picked(nodes[0], block)
            for node in nodes[1:]:
                total = total + picked(node, block)
            win[which, pl.ds(b * BLOCK_ROWS, BLOCK_ROWS)] = total

        def send(i, carry):
            peer = lax.rem(pcol + i, cols)
            pltpu.make_async_remote_copy(
                src_ref=win.at[which, pl.ds(peer * size, size)], dst_ref=win_in.at[which, i],
                send_sem=win_send.at[which], recv_sem=win_recv.at[which],
                device_id=(prow, peer), device_id_type=MESH,
            ).start()
            return carry

        lax.fori_loop(1, cols, send, 0)
        sent.append((win_in.at[which, pl.ds(1, cols - 1)], win_send.at[which]))

    def spread_window(target):
        which = target - 4
        loads["rhs", target].wait()
        wait_bytes(win_in.at[which, pl.ds(1, cols - 1)], win_recv.at[which])
        mine = pl.ds(pcol * size, size)
        total = win[which, mine]
        for i in range(1, cols):
            total = total + win_in[which, i]
        res[which, mine] = rhs[target, mine] - total
        here = res.at[which, mine]

        def spread(i, carry):
            pltpu.make_async_remote_copy(
                src_ref=here, dst_ref=here,
                send_sem=back_send.at[which], recv_sem=back_recv.at[which],
                device_id=(prow, lax.rem(pcol + i, cols)), device_id_type=MESH,
            ).start()
            return carry

        lax.fori_loop(1, cols, spread, 0)
        sent.append((win_in.at[which, pl.ds(1, cols - 1)], back_send.at[which]))

    def begin_parent(target):
        which = target - 4
        loads["diag", target].wait()
        wait_bytes(win_in.at[which, pl.ds(1, cols - 1)], back_recv.at[which])
        begin_node(target, res.at[which])
        pair_node(target)

    def add_upper(which, nodes, fresh):
        count = upper.shape[3] // BLOCK_ROWS

        def one(j, carry):
            block = SUPERNODES * super_blocks + prow * 16 + j
            total = picked(nodes[0], block)
            for node in nodes[1:]:
                total = total + picked(node, block)
            place = j // count
            part = pl.ds((j % count) * BLOCK_ROWS, BLOCK_ROWS)
            spot = (which, place // side, place % side, part)
            upper[spot] = total if fresh else upper[spot] + total
            return carry

        lax.fori_loop(0, cols * count, one, 0)

    up_rows = upper.shape[3] // 2
    chunks = 2
    piece = up_rows // chunks
    chunk_of = [pl.ds(i * piece, piece) for i in range(2 * chunks)]

    def send_upper(which, chunk):
        for i in range(1, side):
            peer_x, peer_y = lax.rem(col_x + i, side), lax.rem(col_y + i, side)
            pltpu.make_async_remote_copy(
                src_ref=upper.at[which, peer_x, :, chunk_of[chunk]],
                dst_ref=up_in.at[which, 0, i, :, chunk_of[chunk]],
                send_sem=up_send.at[which, 0, chunk], recv_sem=up_recv.at[which, 0, chunk],
                device_id=(prow, peer_x * side + col_y), device_id_type=MESH,
            ).start()
            pltpu.make_async_remote_copy(
                src_ref=upper.at[which, :, peer_y, chunk_of[chunks + chunk]],
                dst_ref=up_in.at[which, 1, i, :, chunk_of[chunk]],
                send_sem=up_send.at[which, 1, chunk], recv_sem=up_recv.at[which, 1, chunk],
                device_id=(prow, col_x * side + peer_y), device_id_type=MESH,
            ).start()
        for way in range(2):
            sent.append((up_in.at[which, way, pl.ds(1, side - 1), :, chunk_of[chunk]], up_send.at[which, way, chunk]))

    def middle_upper(which, chunk):
        part = chunk_of[chunk]
        for way in range(2):
            wait_bytes(up_in.at[which, way, pl.ds(1, side - 1), :, part], up_recv.at[which, way, chunk])

            def one(j, carry):
                if way == 0:
                    total = upper[which, col_x, j, chunk_of[chunk]]
                else:
                    total = upper[which, j, col_y, chunk_of[chunks + chunk]]
                for i in range(1, side):
                    total = total + up_in[which, way, i, j, part]
                up_mid[which, way, j, part] = total
                return carry

            lax.fori_loop(0, side, one, 0)
            for i in range(1, side):
                if way == 0:
                    place = lax.rem(col_y + i, side)
                    peer = col_x * side + place
                else:
                    place = lax.rem(col_x + i, side)
                    peer = place * side + col_y
                pltpu.make_async_remote_copy(
                    src_ref=up_mid.at[which, way, place, part], dst_ref=up_last.at[which, way, i, part],
                    send_sem=last_send.at[which, way, chunk], recv_sem=last_recv.at[which, way, chunk],
                    device_id=(prow, peer), device_id_type=MESH,
                ).start()
            sent.append((up_last.at[which, way, pl.ds(1, side - 1), part], last_send.at[which, way, chunk]))

    def finish_upper(which, chunk, fresh):
        part = chunk_of[chunk]
        for way in range(2):
            wait_bytes(up_last.at[which, way, pl.ds(1, side - 1), part], last_recv.at[which, way, chunk])
            total = up_mid[which, way, col_y if way == 0 else col_x, part]
            for i in range(1, side):
                total = total + up_last[which, way, i, part]
            goal = chunk_of[way * chunks + chunk]
            up_out[goal] = total if fresh else up_out[goal] + total

    def run():
        for node in range(4):
            loads["rhs", node].wait()
            loads["diag", node].wait()
            begin_node(node, rhs.at[node])
            if node == 0:
                pl.semaphore_wait(barrier, chips + cols - 1)
            pair_node(node)
        yield
        for node in range(4):
            scatter_node(node)
        for node in range(SUPERNODES):
            prod[node, 8] = jnp.zeros((BLOCK_ROWS, prod.shape[3]), F32)
        for node in range(SUPERNODES):
            split_panel(node)
        yield
        for node in range(4):
            gather_node(node)
        yield
        for parent in (4, 5):
            children = (2 * parent - 8, 2 * parent - 7)
            for node in children:
                share_node(node)
            for node in children:
                multiply_node(node)
            send_window(parent, children)
            yield
        spread_window(4)
        spread_window(5)
        yield
        stores = [store_node(node) for node in range(4)]
        add_upper(0, (0, 1, 2, 3), True)
        begin_parent(4)
        begin_parent(5)
        yield
        scatter_node(4)
        scatter_node(5)
        for chunk in range(chunks):
            send_upper(0, chunk)
        gather_node(4)
        gather_node(5)
        yield
        share_node(4)
        share_node(5)
        multiply_node(4)
        multiply_node(5)
        send_window(6, (0, 1, 2, 3, 4, 5))
        yield
        stores += [store_node(node) for node in (4, 5)]
        add_upper(1, (4, 5), True)
        spread_window(6)
        begin_parent(6)
        scatter_node(6)
        for chunk in range(chunks):
            middle_upper(0, chunk)
        gather_node(6)
        yield
        share_node(6)
        multiply_node(6)
        add_upper(1, (6,), False)
        for chunk in range(chunks):
            send_upper(1, chunk)
        yield
        stores.append(store_node(6))
        for chunk in range(chunks):
            finish_upper(0, chunk, True)
        for chunk in range(chunks):
            middle_upper(1, chunk)
        for chunk in range(chunks):
            finish_upper(1, chunk, False)
        last = pltpu.make_async_copy(up_out, up_hbm, out_sem.at[7])
        last.start()
        for copy in stores:
            copy.wait()
        last.wait()

    for _ in run():
        pass
    for ref, sem in sent:
        wait_bytes(ref, sem)


def copy_out(sol_ref, up_ref, sol_out, up_out, sems):
    copies = [
        pltpu.make_async_copy(sol_ref.at[k], sol_out.at[k], sems.at[k]) for k in range(SUPERNODES)
    ]
    copies.append(pltpu.make_async_copy(up_ref, up_out, sems.at[SUPERNODES]))
    for copy in copies:
        copy.start()
    for copy in copies:
        copy.wait()


def per_device(chips, side, super_blocks, right_side, inverse_diag, panels, block_rows):
    rhs_cols = right_side.shape[2]
    order = right_side.shape[1]
    upper_own = 2 * block_rows.shape[1]
    rows = BLOCK_ROWS // chips
    cols = side * side
    own_upper = upper_own * BLOCK_ROWS // cols
    dma = pltpu.SemaphoreType.DMA
    scratch = [
        pltpu.VMEM((7, order, rhs_cols), F32),
        pltpu.VMEM((7, order, order), F32),
        pltpu.VMEM(panels.shape, F32),
        pltpu.VMEM(panels.shape, BF16),
        pltpu.VMEM(panels.shape, BF16),
        pltpu.VMEM((7, order, rhs_cols), F32),
        pltpu.VMEM((7, BLOCK_ROWS, rhs_cols), F32),
        pltpu.VMEM((7, BLOCK_ROWS, rhs_cols), F32),
        pltpu.VMEM((7, chips, rows, rhs_cols), F32),
        pltpu.VMEM((7, order, rhs_cols), F32),
        pltpu.VMEM((7, 9, BLOCK_ROWS, rhs_cols), F32),
        pltpu.VMEM((3, order, rhs_cols), F32),
        pltpu.VMEM((3, cols, order // cols, rhs_cols), F32),
        pltpu.VMEM((3, order, rhs_cols), F32),
        pltpu.VMEM((2, side, side, own_upper, rhs_cols), F32),
        pltpu.VMEM((2, 2, side, side, own_upper // 2, rhs_cols), F32),
        pltpu.VMEM((2, 2, side, own_upper // 2, rhs_cols), F32),
        pltpu.VMEM((2, 2, side, own_upper // 2, rhs_cols), F32),
        pltpu.VMEM((own_upper, rhs_cols), F32),
        dma((7,)), dma((7,)), dma((7,)), dma((7,)), dma((7,)), dma((7,)), dma((7,)),
        dma((7,)), dma((7,)), dma((7,)), dma((7,)), dma((3,)), dma((3,)), dma((3,)), dma((3,)),
        dma((2, 2, 2)), dma((2, 2, 2)), dma((2, 2, 2)), dma((2, 2, 2)), dma((8,)),
    ]
    anywhere = pl.BlockSpec(memory_space=pl.ANY)
    shapes = (
        jax.ShapeDtypeStruct((7, order, rhs_cols), F32),
        jax.ShapeDtypeStruct((own_upper, rhs_cols), F32),
    )
    results = pl.pallas_call(
        functools.partial(kernel, chips, side, super_blocks),
        out_shape=shapes,
        in_specs=[pl.BlockSpec(memory_space=pltpu.SMEM), anywhere, anywhere, anywhere],
        out_specs=(anywhere, anywhere),
        scratch_shapes=scratch,
        compiler_params=pltpu.CompilerParams(
            collective_id=0, has_side_effects=True, vmem_limit_bytes=58 * 1024 * 1024
        ),
    )(block_rows, right_side, inverse_diag, panels)
    return pl.pallas_call(
        copy_out,
        out_shape=shapes,
        in_specs=[anywhere, anywhere],
        out_specs=(anywhere, anywhere),
        scratch_shapes=[dma((8,))],
    )(*results)


def solution(mesh):
    chips, side = mesh.shape["prow"] // 2, math.isqrt(mesh.shape["pcol"])
    super_blocks = 2 * mesh.shape["prow"]
    in_specs = (
        P(None, "prow", None),
        P(None, "pcol", "prow"),
        P(None, "prow", "pcol"),
        P(None, "prow"),
    )
    out_specs = (P(None, "pcol", None), P(("prow", "pcol"), None))
    return jax.shard_map(
        functools.partial(per_device, chips, side, super_blocks),
        mesh=mesh, in_specs=in_specs, out_specs=out_specs, check_vma=False,
    )
```

```python
import functools
import math

import jax
import jax.numpy as jnp
from jax import lax
from jax.experimental import pallas as pl
from jax.experimental.pallas import tpu as pltpu
from jax.sharding import PartitionSpec as P

BLOCK_ROWS = 128
SUPER_BLOCKS = 32
SUPERNODES = 7
MESH = pl.DeviceIdType.MESH
F32 = jnp.float32
BF16 = jnp.bfloat16


def split(value):
    high = value.astype(BF16)
    low = (value - high.astype(F32)).astype(BF16)
    return high, low


def dot3(a_high, a_low, b_high, b_low):
    dot = functools.partial(jnp.dot, preferred_element_type=F32)
    return dot(a_high, b_high) + (dot(a_high, b_low) + dot(a_low, b_high))


def wait_bytes(ref, sem):
    pltpu.make_async_copy(ref, ref, sem).wait()


def kernel(
    chips, side, super_blocks, rows_ref, rhs_hbm, diag_hbm, panel_hbm, sol_hbm, up_hbm,
    rhs, diag, panel, panel_high, panel_low, terms, pair_in, half, ring_in, xs, prod,
    win, win_in, res, upper, up_in, up_mid, up_last, up_out,
    rhs_sem, diag_sem, panel_sem, pair_send, pair_recv, ring_send, ring_recv,
    gather_send, gather_recv, share_send, share_recv, win_send, win_recv, back_send, back_recv,
    up_send, up_recv, last_send, last_recv, out_sem,
):
    cols = side * side
    prow = lax.axis_index("prow")
    pcol = lax.axis_index("pcol")
    chip, core = prow // 2, prow % 2
    col_x, col_y = pcol // side, pcol % side
    other = chip * 2 + 1 - core
    own_half, other_half = core * BLOCK_ROWS, (1 - core) * BLOCK_ROWS
    rows = BLOCK_ROWS // chips
    own_rows = own_half + chip * rows
    sent = []

    barrier = pltpu.get_barrier_semaphore()
    pl.semaphore_signal(barrier, inc=1, device_id=(other, pcol), device_id_type=MESH)

    def greet_chip(i, carry):
        peer = lax.rem(chip + i, chips) * 2 + core
        pl.semaphore_signal(barrier, inc=1, device_id=(peer, pcol), device_id_type=MESH)
        return carry

    def greet_col(i, carry):
        pl.semaphore_signal(
            barrier, inc=1, device_id=(prow, lax.rem(pcol + i, cols)), device_id_type=MESH
        )
        return carry

    lax.fori_loop(1, chips, greet_chip, 0)
    lax.fori_loop(1, cols, greet_col, 0)

    loads = {}
    for k in range(SUPERNODES):
        loads["rhs", k] = pltpu.make_async_copy(rhs_hbm.at[k], rhs.at[k], rhs_sem.at[k])
        loads["diag", k] = pltpu.make_async_copy(diag_hbm.at[k], diag.at[k], diag_sem.at[k])
        loads["panel", k] = pltpu.make_async_copy(panel_hbm.at[k], panel.at[k], panel_sem.at[k])
    for k in range(4):
        loads["rhs", k].start()
        loads["diag", k].start()
    for k in range(SUPERNODES):
        if k >= 4:
            loads["rhs", k].start()
            loads["diag", k].start()
        loads["panel", k].start()

    def begin_node(node, residual):
        d_high, d_low = split(diag[node])
        r_high, r_low = split(residual[...])
        terms[node] = dot3(d_high, d_low, r_high, r_low)

    def pair_node(node):
        pltpu.make_async_remote_copy(
            src_ref=terms.at[node, pl.ds(other_half, BLOCK_ROWS)], dst_ref=pair_in.at[node],
            send_sem=pair_send.at[node], recv_sem=pair_recv.at[node],
            device_id=(other, pcol), device_id_type=MESH,
        ).start()
        sent.append((pair_in.at[node], pair_send.at[node]))

    def scatter_node(node):
        wait_bytes(pair_in.at[node], pair_recv.at[node])
        half[node] = terms[node, pl.ds(own_half, BLOCK_ROWS)] + pair_in[node]

        def send(i, inner):
            peer = lax.rem(chip + i, chips)
            pltpu.make_async_remote_copy(
                src_ref=half.at[node, pl.ds(peer * rows, rows)], dst_ref=ring_in.at[node, i],
                send_sem=ring_send.at[node], recv_sem=ring_recv.at[node],
                device_id=(peer * 2 + core, pcol), device_id_type=MESH,
            ).start()
            return inner

        lax.fori_loop(1, chips, send, 0)
        sent.append((ring_in.at[node, pl.ds(1, chips - 1)], ring_send.at[node]))

    def gather_node(node):
        wait_bytes(ring_in.at[node, pl.ds(1, chips - 1)], ring_recv.at[node])
        total = half[node, pl.ds(chip * rows, rows)]
        for i in range(1, chips):
            total = total + ring_in[node, i]
        xs[node, pl.ds(own_rows, rows)] = total
        here = xs.at[node, pl.ds(own_rows, rows)]

        def send(i, inner):
            peer = lax.rem(chip + i, chips)
            pltpu.make_async_remote_copy(
                src_ref=here, dst_ref=here,
                send_sem=gather_send.at[node], recv_sem=gather_recv.at[node],
                device_id=(peer * 2 + core, pcol), device_id_type=MESH,
            ).start()
            return inner

        lax.fori_loop(1, chips, send, 0)
        sent.append((ring_in.at[node, pl.ds(1, chips - 1)], gather_send.at[node]))

    def share_node(node):
        wait_bytes(ring_in.at[node, pl.ds(1, chips - 1)], gather_recv.at[node])
        here = xs.at[node, pl.ds(own_half, BLOCK_ROWS)]
        pltpu.make_async_remote_copy(
            src_ref=here, dst_ref=here,
            send_sem=share_send.at[node], recv_sem=share_recv.at[node],
            device_id=(other, pcol), device_id_type=MESH,
        ).start()
        sent.append((pair_in.at[node], share_send.at[node]))

    def multiply_node(node):
        wait_bytes(xs.at[node, pl.ds(other_half, BLOCK_ROWS)], share_recv.at[node])
        x_high, x_low = split(xs[node])

        product = dot3(panel_high[node], panel_low[node], x_high, x_low)
        for slot in range(8):
            prod[node, slot] = product[slot * BLOCK_ROWS:(slot + 1) * BLOCK_ROWS]

    def store_node(node):
        copy = pltpu.make_async_copy(xs.at[node], sol_hbm.at[node], out_sem.at[node])
        copy.start()
        return copy

    def split_panel(node):
        loads["panel", node].wait()

        def one(step, carry):
            part = pl.ds(step * BLOCK_ROWS, BLOCK_ROWS)
            panel_high[node, part], panel_low[node, part] = split(panel[node, part])
            return carry

        lax.fori_loop(0, 8, one, 0)

    def picked(node, block):
        slot = 8
        for i in range(8):
            slot = jnp.where(rows_ref[node, i] == block, i, slot)
        return prod[node, slot]

    size = 2 * BLOCK_ROWS // cols

    def send_window(target, nodes):
        which = target - 4
        for b in range(2):
            block = target * super_blocks + prow * 2 + b
            total = picked(nodes[0], block)
            for node in nodes[1:]:
                total = total + picked(node, block)
            win[which, pl.ds(b * BLOCK_ROWS, BLOCK_ROWS)] = total

        def send(i, carry):
            peer = lax.rem(pcol + i, cols)
            pltpu.make_async_remote_copy(
                src_ref=win.at[which, pl.ds(peer * size, size)], dst_ref=win_in.at[which, i],
                send_sem=win_send.at[which], recv_sem=win_recv.at[which],
                device_id=(prow, peer), device_id_type=MESH,
            ).start()
            return carry

        lax.fori_loop(1, cols, send, 0)
        sent.append((win_in.at[which, pl.ds(1, cols - 1)], win_send.at[which]))

    def spread_window(target):
        which = target - 4
        loads["rhs", target].wait()
        wait_bytes(win_in.at[which, pl.ds(1, cols - 1)], win_recv.at[which])
        mine = pl.ds(pcol * size, size)
        total = win[which, mine]
        for i in range(1, cols):
            total = total + win_in[which, i]
        res[which, mine] = rhs[target, mine] - total
        here = res.at[which, mine]

        def spread(i, carry):
            pltpu.make_async_remote_copy(
                src_ref=here, dst_ref=here,
                send_sem=back_send.at[which], recv_sem=back_recv.at[which],
                device_id=(prow, lax.rem(pcol + i, cols)), device_id_type=MESH,
            ).start()
            return carry

        lax.fori_loop(1, cols, spread, 0)
        sent.append((win_in.at[which, pl.ds(1, cols - 1)], back_send.at[which]))

    def begin_parent(target):
        which = target - 4
        loads["diag", target].wait()
        wait_bytes(win_in.at[which, pl.ds(1, cols - 1)], back_recv.at[which])
        begin_node(target, res.at[which])
        pair_node(target)

    def add_upper(which, nodes, fresh):
        count = upper.shape[3] // BLOCK_ROWS

        def one(j, carry):
            block = SUPERNODES * super_blocks + prow * 16 + j
            total = picked(nodes[0], block)
            for node in nodes[1:]:
                total = total + picked(node, block)
            place = j // count
            part = pl.ds((j % count) * BLOCK_ROWS, BLOCK_ROWS)
            spot = (which, place // side, place % side, part)
            upper[spot] = total if fresh else upper[spot] + total
            return carry

        lax.fori_loop(0, cols * count, one, 0)

    up_rows = upper.shape[3] // 2
    chunks = 2
    piece = up_rows // chunks
    chunk_of = [pl.ds(i * piece, piece) for i in range(2 * chunks)]

    def send_upper(which, chunk):
        for i in range(1, side):
            peer_x, peer_y = lax.rem(col_x + i, side), lax.rem(col_y + i, side)
            pltpu.make_async_remote_copy(
                src_ref=upper.at[which, peer_x, :, chunk_of[chunk]],
                dst_ref=up_in.at[which, 0, i, :, chunk_of[chunk]],
                send_sem=up_send.at[which, 0, chunk], recv_sem=up_recv.at[which, 0, chunk],
                device_id=(prow, peer_x * side + col_y), device_id_type=MESH,
            ).start()
            pltpu.make_async_remote_copy(
                src_ref=upper.at[which, :, peer_y, chunk_of[chunks + chunk]],
                dst_ref=up_in.at[which, 1, i, :, chunk_of[chunk]],
                send_sem=up_send.at[which, 1, chunk], recv_sem=up_recv.at[which, 1, chunk],
                device_id=(prow, col_x * side + peer_y), device_id_type=MESH,
            ).start()
        for way in range(2):
            sent.append((up_in.at[which, way, pl.ds(1, side - 1), :, chunk_of[chunk]], up_send.at[which, way, chunk]))

    def middle_upper(which, chunk):
        part = chunk_of[chunk]
        for way in range(2):
            wait_bytes(up_in.at[which, way, pl.ds(1, side - 1), :, part], up_recv.at[which, way, chunk])

            def one(j, carry):
                if way == 0:
                    total = upper[which, col_x, j, chunk_of[chunk]]
                else:
                    total = upper[which, j, col_y, chunk_of[chunks + chunk]]
                for i in range(1, side):
                    total = total + up_in[which, way, i, j, part]
                up_mid[which, way, j, part] = total
                return carry

            lax.fori_loop(0, side, one, 0)
            for i in range(1, side):
                if way == 0:
                    place = lax.rem(col_y + i, side)
                    peer = col_x * side + place
                else:
                    place = lax.rem(col_x + i, side)
                    peer = place * side + col_y
                pltpu.make_async_remote_copy(
                    src_ref=up_mid.at[which, way, place, part], dst_ref=up_last.at[which, way, i, part],
                    send_sem=last_send.at[which, way, chunk], recv_sem=last_recv.at[which, way, chunk],
                    device_id=(prow, peer), device_id_type=MESH,
                ).start()
            sent.append((up_last.at[which, way, pl.ds(1, side - 1), part], last_send.at[which, way, chunk]))

    def finish_upper(which, chunk, fresh):
        part = chunk_of[chunk]
        for way in range(2):
            wait_bytes(up_last.at[which, way, pl.ds(1, side - 1), part], last_recv.at[which, way, chunk])
            total = up_mid[which, way, col_y if way == 0 else col_x, part]
            for i in range(1, side):
                total = total + up_last[which, way, i, part]
            goal = chunk_of[way * chunks + chunk]
            up_out[goal] = total if fresh else up_out[goal] + total

    def run():
        for node in range(4):
            loads["rhs", node].wait()
            loads["diag", node].wait()
            begin_node(node, rhs.at[node])
            if node == 0:
                pl.semaphore_wait(barrier, chips + cols - 1)
            pair_node(node)
        yield
        for node in range(4):
            scatter_node(node)
        for node in range(SUPERNODES):
            prod[node, 8] = jnp.zeros((BLOCK_ROWS, prod.shape[3]), F32)
        for node in range(SUPERNODES):
            split_panel(node)
        yield
        for node in range(4):
            gather_node(node)
        yield
        for parent in (4, 5):
            children = (2 * parent - 8, 2 * parent - 7)
            for node in children:
                share_node(node)
            for node in children:
                multiply_node(node)
            send_window(parent, children)
            yield
        spread_window(4)
        spread_window(5)
        yield
        stores = [store_node(node) for node in range(4)]
        add_upper(0, (0, 1, 2, 3), True)
        begin_parent(4)
        begin_parent(5)
        yield
        scatter_node(4)
        scatter_node(5)
        for chunk in range(chunks):
            send_upper(0, chunk)
        gather_node(4)
        gather_node(5)
        yield
        share_node(4)
        share_node(5)
        multiply_node(4)
        multiply_node(5)
        send_window(6, (0, 1, 2, 3, 4, 5))
        yield
        stores += [store_node(node) for node in (4, 5)]
        add_upper(1, (4, 5), True)
        spread_window(6)
        begin_parent(6)
        scatter_node(6)
        for chunk in range(chunks):
            middle_upper(0, chunk)
        gather_node(6)
        yield
        share_node(6)
        multiply_node(6)
        add_upper(1, (6,), False)
        for chunk in range(chunks):
            send_upper(1, chunk)
        yield
        stores.append(store_node(6))
        for chunk in range(chunks):
            finish_upper(0, chunk, True)
        for chunk in range(chunks):
            middle_upper(1, chunk)
        for chunk in range(chunks):
            finish_upper(1, chunk, False)
        last = pltpu.make_async_copy(up_out, up_hbm, out_sem.at[7])
        last.start()
        for copy in stores:
            copy.wait()
        last.wait()

    for _ in run():
        pass
    for ref, sem in sent:
        wait_bytes(ref, sem)


def copy_out(sol_ref, up_ref, sol_out, up_out, sems):
    copies = [
        pltpu.make_async_copy(sol_ref.at[k], sol_out.at[k], sems.at[k]) for k in range(SUPERNODES)
    ]
    copies.append(pltpu.make_async_copy(up_ref, up_out, sems.at[SUPERNODES]))
    for copy in copies:
        copy.start()
    for copy in copies:
        copy.wait()


def per_device(chips, side, super_blocks, right_side, inverse_diag, panels, block_rows):
    rhs_cols = right_side.shape[2]
    order = right_side.shape[1]
    upper_own = 2 * block_rows.shape[1]
    rows = BLOCK_ROWS // chips
    cols = side * side
    own_upper = upper_own * BLOCK_ROWS // cols
    dma = pltpu.SemaphoreType.DMA
    scratch = [
        pltpu.VMEM((7, order, rhs_cols), F32),
        pltpu.VMEM((7, order, order), F32),
        pltpu.VMEM(panels.shape, F32),
        pltpu.VMEM(panels.shape, BF16),
        pltpu.VMEM(panels.shape, BF16),
        pltpu.VMEM((7, order, rhs_cols), F32),
        pltpu.VMEM((7, BLOCK_ROWS, rhs_cols), F32),
        pltpu.VMEM((7, BLOCK_ROWS, rhs_cols), F32),
        pltpu.VMEM((7, chips, rows, rhs_cols), F32),
        pltpu.VMEM((7, order, rhs_cols), F32),
        pltpu.VMEM((7, 9, BLOCK_ROWS, rhs_cols), F32),
        pltpu.VMEM((3, order, rhs_cols), F32),
        pltpu.VMEM((3, cols, order // cols, rhs_cols), F32),
        pltpu.VMEM((3, order, rhs_cols), F32),
        pltpu.VMEM((2, side, side, own_upper, rhs_cols), F32),
        pltpu.VMEM((2, 2, side, side, own_upper // 2, rhs_cols), F32),
        pltpu.VMEM((2, 2, side, own_upper // 2, rhs_cols), F32),
        pltpu.VMEM((2, 2, side, own_upper // 2, rhs_cols), F32),
        pltpu.VMEM((own_upper, rhs_cols), F32),
        dma((7,)), dma((7,)), dma((7,)), dma((7,)), dma((7,)), dma((7,)), dma((7,)),
        dma((7,)), dma((7,)), dma((7,)), dma((7,)), dma((3,)), dma((3,)), dma((3,)), dma((3,)),
        dma((2, 2, 2)), dma((2, 2, 2)), dma((2, 2, 2)), dma((2, 2, 2)), dma((8,)),
    ]
    anywhere = pl.BlockSpec(memory_space=pl.ANY)
    stay = pl.BlockSpec(memory_space=pltpu.HBM)
    shapes = (
        jax.ShapeDtypeStruct((7, order, rhs_cols), F32),
        jax.ShapeDtypeStruct((own_upper, rhs_cols), F32),
    )
    results = pl.pallas_call(
        functools.partial(kernel, chips, side, super_blocks),
        out_shape=shapes,
        in_specs=[pl.BlockSpec(memory_space=pltpu.SMEM), stay, stay, stay],
        out_specs=(anywhere, anywhere),
        scratch_shapes=scratch,
        compiler_params=pltpu.CompilerParams(
            collective_id=0, has_side_effects=True, vmem_limit_bytes=52 * 1024 * 1024
        ),
    )(block_rows, right_side, inverse_diag, panels)
    return pl.pallas_call(
        copy_out,
        out_shape=shapes,
        in_specs=[pl.BlockSpec(memory_space=pltpu.VMEM)] * 2,
        out_specs=(stay, stay),
        scratch_shapes=[dma((8,))],
        compiler_params=pltpu.CompilerParams(vmem_limit_bytes=8 * 1024 * 1024),
    )(*results)


def solution(mesh):
    chips, side = mesh.shape["prow"] // 2, math.isqrt(mesh.shape["pcol"])
    super_blocks = 2 * mesh.shape["prow"]
    in_specs = (
        P(None, "prow", None),
        P(None, "pcol", "prow"),
        P(None, "prow", "pcol"),
        P(None, "prow"),
    )
    out_specs = (P(None, "pcol", None), P(("prow", "pcol"), None))
    return jax.shard_map(
        functools.partial(per_device, chips, side, super_blocks),
        mesh=mesh, in_specs=in_specs, out_specs=out_specs, check_vma=False,
    )
```

```python
import functools
import math

import jax
import jax.numpy as jnp
from jax import lax
from jax.experimental import pallas as pl
from jax.experimental.pallas import tpu as pltpu
from jax.sharding import PartitionSpec as P

BLOCK_ROWS = 128
SUPER_BLOCKS = 32
SUPERNODES = 7
LEVELS = ((0, 4), (4, 2), (6, 1))
MESH = pl.DeviceIdType.MESH
F32 = jnp.float32
BF16 = jnp.bfloat16


def split(value):
    high = value.astype(BF16)
    low = (value - high.astype(F32)).astype(BF16)
    return high, low


def dot3(a_high, a_low, b_high, b_low):
    dot = functools.partial(jnp.dot, preferred_element_type=F32)
    return dot(a_high, b_high) + (dot(a_high, b_low) + dot(a_low, b_high))


def wait_bytes(ref, sem):
    pltpu.make_async_copy(ref, ref, sem).wait()


def kernel(
    chips, side, super_blocks, rows_ref, rhs_hbm, diag_hbm, panel_hbm, sol_hbm, up_hbm,
    rhs, diag, diag_high, diag_low, panel, panel_high, panel_low, terms, pair_in, half, ring_in, xs,
    prod, win, win_in, res, upper, up_in, up_mid, up_last, up_out,
    rhs_sem, diag_sem, panel_sem, pair_send, pair_recv, ring_send, ring_recv,
    gather_send, gather_recv, share_send, share_recv, win_send, win_recv, back_send, back_recv,
    up_send, up_recv, last_send, last_recv, out_sem,
):
    cols = side * side
    width = rhs.shape[3]
    prow = lax.axis_index("prow")
    pcol = lax.axis_index("pcol")
    chip, core = prow // 2, prow % 2
    col_x, col_y = pcol // side, pcol % side
    other = chip * 2 + 1 - core
    own_half, other_half = core * BLOCK_ROWS, (1 - core) * BLOCK_ROWS
    rows = BLOCK_ROWS // chips
    own_rows = own_half + chip * rows
    sent = []

    barrier = pltpu.get_barrier_semaphore()
    pl.semaphore_signal(barrier, inc=1, device_id=(other, pcol), device_id_type=MESH)

    def greet_chip(i, carry):
        peer = lax.rem(chip + i, chips) * 2 + core
        pl.semaphore_signal(barrier, inc=1, device_id=(peer, pcol), device_id_type=MESH)
        return carry

    def greet_col(i, carry):
        pl.semaphore_signal(
            barrier, inc=1, device_id=(prow, lax.rem(pcol + i, cols)), device_id_type=MESH
        )
        return carry

    lax.fori_loop(1, chips, greet_chip, 0)
    lax.fori_loop(1, cols, greet_col, 0)

    loads = {}
    for h in range(2):
        part = pl.ds(h * width, width)
        for level, (first, count) in enumerate(LEVELS):
            nodes = pl.ds(first, count)
            loads["rhs", h, level] = pltpu.make_async_copy(
                rhs_hbm.at[nodes, :, part], rhs.at[h, nodes], rhs_sem.at[h, level]
            )
    for k in range(SUPERNODES):
        loads["diag", k] = pltpu.make_async_copy(diag_hbm.at[k], diag.at[k], diag_sem.at[k])
        loads["panel", k] = pltpu.make_async_copy(panel_hbm.at[k], panel.at[k], panel_sem.at[k])
    loads["rhs", 0, 0].start()
    for k in range(4):
        loads["diag", k].start()
    loads["rhs", 1, 0].start()
    for k in range(4):
        loads["panel", k].start()
    for h in range(2):
        for level in (1, 2):
            loads["rhs", h, level].start()
    for k in range(4, SUPERNODES):
        loads["diag", k].start()
        loads["panel", k].start()

    def nodes_of(level):
        return pl.ds(*LEVELS[level])

    def each(level):
        first, count = LEVELS[level]
        return range(first, first + count)

    def split_diag(node):
        loads["diag", node].wait()
        diag_high[node], diag_low[node] = split(diag[node])

    def begin(level, h):
        for node in each(level):
            residual = rhs[h, node] if level == 0 else res[h, node - 4]
            r_high, r_low = split(residual)
            terms[h, node] = dot3(diag_high[node], diag_low[node], r_high, r_low)

    def pair(level, h):
        nodes = nodes_of(level)
        pltpu.make_async_remote_copy(
            src_ref=terms.at[h, nodes, pl.ds(other_half, BLOCK_ROWS)], dst_ref=pair_in.at[h, nodes],
            send_sem=pair_send.at[h, level], recv_sem=pair_recv.at[h, level],
            device_id=(other, pcol), device_id_type=MESH,
        ).start()
        sent.append((pair_in.at[h, nodes], pair_send.at[h, level]))

    def scatter(level, h):
        nodes = nodes_of(level)
        wait_bytes(pair_in.at[h, nodes], pair_recv.at[h, level])
        for node in each(level):
            half[h, node] = terms[h, node, pl.ds(own_half, BLOCK_ROWS)] + pair_in[h, node]

        def send(i, carry):
            peer = lax.rem(chip + i, chips)
            pltpu.make_async_remote_copy(
                src_ref=half.at[h, nodes, pl.ds(peer * rows, rows)], dst_ref=ring_in.at[h, i, nodes],
                send_sem=ring_send.at[h, level], recv_sem=ring_recv.at[h, level],
                device_id=(peer * 2 + core, pcol), device_id_type=MESH,
            ).start()
            return carry

        lax.fori_loop(1, chips, send, 0)
        sent.append((ring_in.at[h, pl.ds(1, chips - 1), nodes], ring_send.at[h, level]))

    def gather(level, h):
        nodes = nodes_of(level)
        wait_bytes(ring_in.at[h, pl.ds(1, chips - 1), nodes], ring_recv.at[h, level])
        for node in each(level):
            total = half[h, node, pl.ds(chip * rows, rows)]
            for i in range(1, chips):
                total = total + ring_in[h, i, node]
            xs[h, node, pl.ds(own_rows, rows)] = total
        here = xs.at[h, nodes, pl.ds(own_rows, rows)]

        def send(i, carry):
            peer = lax.rem(chip + i, chips)
            pltpu.make_async_remote_copy(
                src_ref=here, dst_ref=here,
                send_sem=gather_send.at[h, level], recv_sem=gather_recv.at[h, level],
                device_id=(peer * 2 + core, pcol), device_id_type=MESH,
            ).start()
            return carry

        lax.fori_loop(1, chips, send, 0)
        sent.append((ring_in.at[h, pl.ds(1, chips - 1), nodes], gather_send.at[h, level]))

    def share(level, h):
        nodes = nodes_of(level)
        wait_bytes(ring_in.at[h, pl.ds(1, chips - 1), nodes], gather_recv.at[h, level])
        here = xs.at[h, nodes, pl.ds(own_half, BLOCK_ROWS)]
        pltpu.make_async_remote_copy(
            src_ref=here, dst_ref=here,
            send_sem=share_send.at[h, level], recv_sem=share_recv.at[h, level],
            device_id=(other, pcol), device_id_type=MESH,
        ).start()
        sent.append((pair_in.at[h, nodes], share_send.at[h, level]))

    def multiply(level, h):
        wait_bytes(pair_in.at[h, nodes_of(level)], share_recv.at[h, level])
        for node in each(level):
            x_high, x_low = split(xs[h, node])
            product = dot3(panel_high[node], panel_low[node], x_high, x_low)
            for slot in range(8):
                prod[h, node, slot] = product[slot * BLOCK_ROWS:(slot + 1) * BLOCK_ROWS]

    def store(level, h):
        copy = pltpu.make_async_copy(
            xs.at[h, nodes_of(level)], sol_hbm.at[nodes_of(level), :, pl.ds(h * width, width)],
            out_sem.at[h, level],
        )
        copy.start()
        return copy

    def split_panel(node):
        loads["panel", node].wait()

        def one(step, carry):
            part = pl.ds(step * BLOCK_ROWS, BLOCK_ROWS)
            panel_high[node, part], panel_low[node, part] = split(panel[node, part])
            return carry

        lax.fori_loop(0, 8, one, 0)

    def picked(h, node, block):
        slot = 8
        for i in range(8):
            slot = jnp.where(rows_ref[node, i] == block, i, slot)
        return prod[h, node, slot]

    size = 2 * BLOCK_ROWS // cols
    windows = (pl.ds(0, 2), pl.ds(2, 1))
    targets = (((4, (0, 1)), (5, (2, 3))), ((6, (0, 1, 2, 3, 4, 5)),))

    def send_window(level, h):
        which = windows[level]
        for target, children in targets[level]:
            for b in range(2):
                block = target * super_blocks + prow * 2 + b
                total = picked(h, children[0], block)
                for node in children[1:]:
                    total = total + picked(h, node, block)
                win[h, target - 4, pl.ds(b * BLOCK_ROWS, BLOCK_ROWS)] = total

        def send(i, carry):
            peer = lax.rem(pcol + i, cols)
            pltpu.make_async_remote_copy(
                src_ref=win.at[h, which, pl.ds(peer * size, size)], dst_ref=win_in.at[h, i, which],
                send_sem=win_send.at[h, level], recv_sem=win_recv.at[h, level],
                device_id=(prow, peer), device_id_type=MESH,
            ).start()
            return carry

        lax.fori_loop(1, cols, send, 0)
        sent.append((win_in.at[h, pl.ds(1, cols - 1), which], win_send.at[h, level]))

    def spread(level, h):
        which = windows[level]
        loads["rhs", h, level + 1].wait()
        wait_bytes(win_in.at[h, pl.ds(1, cols - 1), which], win_recv.at[h, level])
        mine = pl.ds(pcol * size, size)
        for target, _ in targets[level]:
            total = win[h, target - 4, mine]
            for i in range(1, cols):
                total = total + win_in[h, i, target - 4]
            res[h, target - 4, mine] = rhs[h, target, mine] - total
        here = res.at[h, which, mine]

        def send(i, carry):
            pltpu.make_async_remote_copy(
                src_ref=here, dst_ref=here,
                send_sem=back_send.at[h, level], recv_sem=back_recv.at[h, level],
                device_id=(prow, lax.rem(pcol + i, cols)), device_id_type=MESH,
            ).start()
            return carry

        lax.fori_loop(1, cols, send, 0)
        sent.append((win_in.at[h, pl.ds(1, cols - 1), which], back_send.at[h, level]))

    def begin_next(level, h):
        wait_bytes(win_in.at[h, pl.ds(1, cols - 1), windows[level - 1]], back_recv.at[h, level - 1])
        begin(level, h)
        pair(level, h)

    def add_upper(which, h, nodes, fresh):
        count = upper.shape[4] // BLOCK_ROWS

        def one(j, carry):
            block = SUPERNODES * super_blocks + prow * 16 + j
            total = picked(h, nodes[0], block)
            for node in nodes[1:]:
                total = total + picked(h, node, block)
            place = j // count
            part = pl.ds((j % count) * BLOCK_ROWS, BLOCK_ROWS)
            spot = (which, h, place // side, place % side, part)
            upper[spot] = total if fresh else upper[spot] + total
            return carry

        lax.fori_loop(0, cols * count, one, 0)

    up_rows = upper.shape[4] // 2
    row_half = (pl.ds(0, up_rows), pl.ds(up_rows, up_rows))

    def send_upper(which, h):
        for i in range(1, side):
            peer_x, peer_y = lax.rem(col_x + i, side), lax.rem(col_y + i, side)
            pltpu.make_async_remote_copy(
                src_ref=upper.at[which, h, peer_x, :, row_half[0]], dst_ref=up_in.at[which, h, 0, i],
                send_sem=up_send.at[which, h, 0], recv_sem=up_recv.at[which, h, 0],
                device_id=(prow, peer_x * side + col_y), device_id_type=MESH,
            ).start()
            pltpu.make_async_remote_copy(
                src_ref=upper.at[which, h, :, peer_y, row_half[1]], dst_ref=up_in.at[which, h, 1, i],
                send_sem=up_send.at[which, h, 1], recv_sem=up_recv.at[which, h, 1],
                device_id=(prow, col_x * side + peer_y), device_id_type=MESH,
            ).start()
        for way in range(2):
            sent.append((up_in.at[which, h, way, pl.ds(1, side - 1)], up_send.at[which, h, way]))

    def middle_upper(which, h):
        for way in range(2):
            wait_bytes(up_in.at[which, h, way, pl.ds(1, side - 1)], up_recv.at[which, h, way])

            def one(j, carry):
                if way == 0:
                    total = upper[which, h, col_x, j, row_half[0]]
                else:
                    total = upper[which, h, j, col_y, row_half[1]]
                for i in range(1, side):
                    total = total + up_in[which, h, way, i, j]
                up_mid[which, h, way, j] = total
                return carry

            lax.fori_loop(0, side, one, 0)
            for i in range(1, side):
                if way == 0:
                    place = lax.rem(col_y + i, side)
                    peer = col_x * side + place
                else:
                    place = lax.rem(col_x + i, side)
                    peer = place * side + col_y
                pltpu.make_async_remote_copy(
                    src_ref=up_mid.at[which, h, way, place], dst_ref=up_last.at[which, h, way, i],
                    send_sem=last_send.at[which, h, way], recv_sem=last_recv.at[which, h, way],
                    device_id=(prow, peer), device_id_type=MESH,
                ).start()
            sent.append((up_last.at[which, h, way, pl.ds(1, side - 1)], last_send.at[which, h, way]))

    def finish_upper(which, h, fresh):
        for way in range(2):
            wait_bytes(up_last.at[which, h, way, pl.ds(1, side - 1)], last_recv.at[which, h, way])
            total = up_mid[which, h, way, col_y if way == 0 else col_x]
            for i in range(1, side):
                total = total + up_last[which, h, way, i]
            goal = (row_half[way], pl.ds(h * width, width))
            up_out[goal] = total if fresh else up_out[goal] + total

    def run():
        stores = []
        for h in range(2):
            loads["rhs", h, 0].wait()
            if h == 0:
                for node in range(4):
                    split_diag(node)
            begin(0, h)
            if h == 0:
                pl.semaphore_wait(barrier, chips + cols - 1)
            pair(0, h)
        yield
        for h in range(2):
            scatter(0, h)
        for h in range(2):
            for node in range(SUPERNODES):
                prod[h, node, 8] = jnp.zeros((BLOCK_ROWS, width), F32)
        for node in range(SUPERNODES):
            split_panel(node)
        for node in range(4, SUPERNODES):
            split_diag(node)
        yield
        for h in range(2):
            gather(0, h)
        yield
        for h in range(2):
            share(0, h)
            multiply(0, h)
            send_window(0, h)
        yield
        for h in range(2):
            spread(0, h)
        yield
        for h in range(2):
            stores.append(store(0, h))
            add_upper(0, h, (0, 1, 2, 3), True)
        for h in range(2):
            begin_next(1, h)
        yield
        for h in range(2):
            scatter(1, h)
        for h in range(2):
            send_upper(0, h)
        for h in range(2):
            gather(1, h)
        yield
        for h in range(2):
            share(1, h)
            multiply(1, h)
            send_window(1, h)
        yield
        for h in range(2):
            stores.append(store(1, h))
            add_upper(1, h, (4, 5), True)
        for h in range(2):
            spread(1, h)
        yield
        for h in range(2):
            begin_next(2, h)
        for h in range(2):
            scatter(2, h)
        for h in range(2):
            middle_upper(0, h)
        for h in range(2):
            gather(2, h)
        yield
        for h in range(2):
            share(2, h)
            multiply(2, h)
            add_upper(1, h, (6,), False)
            send_upper(1, h)
        yield
        for h in range(2):
            stores.append(store(2, h))
            finish_upper(0, h, True)
        for h in range(2):
            middle_upper(1, h)
        for h in range(2):
            finish_upper(1, h, False)
        last = pltpu.make_async_copy(up_out, up_hbm, out_sem.at[0, 3])
        last.start()
        for copy in stores:
            copy.wait()
        last.wait()

    for _ in run():
        pass
    for ref, sem in sent:
        wait_bytes(ref, sem)


def copy_out(sol_ref, up_ref, sol_out, up_out, sems):
    copies = [
        pltpu.make_async_copy(sol_ref.at[k], sol_out.at[k], sems.at[k]) for k in range(SUPERNODES)
    ]
    copies.append(pltpu.make_async_copy(up_ref, up_out, sems.at[SUPERNODES]))
    for copy in copies:
        copy.start()
    for copy in copies:
        copy.wait()


def per_device(chips, side, super_blocks, right_side, inverse_diag, panels, block_rows):
    rhs_cols = right_side.shape[2]
    order = right_side.shape[1]
    upper_own = 2 * block_rows.shape[1]
    rows = BLOCK_ROWS // chips
    cols = side * side
    own_upper = upper_own * BLOCK_ROWS // cols
    dma = pltpu.SemaphoreType.DMA
    width = rhs_cols // 2
    scratch = [
        pltpu.VMEM((2, 7, order, width), F32),
        pltpu.VMEM((7, order, order), F32),
        pltpu.VMEM((7, order, order), BF16),
        pltpu.VMEM((7, order, order), BF16),
        pltpu.VMEM(panels.shape, F32),
        pltpu.VMEM(panels.shape, BF16),
        pltpu.VMEM(panels.shape, BF16),
        pltpu.VMEM((2, 7, order, width), F32),
        pltpu.VMEM((2, 7, BLOCK_ROWS, width), F32),
        pltpu.VMEM((2, 7, BLOCK_ROWS, width), F32),
        pltpu.VMEM((2, chips, 7, rows, width), F32),
        pltpu.VMEM((2, 7, order, width), F32),
        pltpu.VMEM((2, 7, 9, BLOCK_ROWS, width), F32),
        pltpu.VMEM((2, 3, order, width), F32),
        pltpu.VMEM((2, cols, 3, order // cols, width), F32),
        pltpu.VMEM((2, 3, order, width), F32),
        pltpu.VMEM((2, 2, side, side, own_upper, width), F32),
        pltpu.VMEM((2, 2, 2, side, side, own_upper // 2, width), F32),
        pltpu.VMEM((2, 2, 2, side, own_upper // 2, width), F32),
        pltpu.VMEM((2, 2, 2, side, own_upper // 2, width), F32),
        pltpu.VMEM((own_upper, rhs_cols), F32),
        dma((2, 3)), dma((7,)), dma((7,)), dma((2, 3)), dma((2, 3)), dma((2, 3)), dma((2, 3)),
        dma((2, 3)), dma((2, 3)), dma((2, 3)), dma((2, 3)), dma((2, 2)), dma((2, 2)), dma((2, 2)), dma((2, 2)),
        dma((2, 2, 2)), dma((2, 2, 2)), dma((2, 2, 2)), dma((2, 2, 2)), dma((2, 4)),
    ]
    anywhere = pl.BlockSpec(memory_space=pl.ANY)
    stay = pl.BlockSpec(memory_space=pltpu.HBM)
    shapes = (
        jax.ShapeDtypeStruct((7, order, rhs_cols), F32),
        jax.ShapeDtypeStruct((own_upper, rhs_cols), F32),
    )
    results = pl.pallas_call(
        functools.partial(kernel, chips, side, super_blocks),
        out_shape=shapes,
        in_specs=[pl.BlockSpec(memory_space=pltpu.SMEM), stay, stay, stay],
        out_specs=(anywhere, anywhere),
        scratch_shapes=scratch,
        compiler_params=pltpu.CompilerParams(
            collective_id=0, has_side_effects=True, vmem_limit_bytes=52 * 1024 * 1024
        ),
    )(block_rows, right_side, inverse_diag, panels)
    return pl.pallas_call(
        copy_out,
        out_shape=shapes,
        in_specs=[pl.BlockSpec(memory_space=pltpu.VMEM)] * 2,
        out_specs=(stay, stay),
        scratch_shapes=[dma((8,))],
        compiler_params=pltpu.CompilerParams(vmem_limit_bytes=8 * 1024 * 1024),
    )(*results)


def solution(mesh):
    chips, side = mesh.shape["prow"] // 2, math.isqrt(mesh.shape["pcol"])
    super_blocks = 2 * mesh.shape["prow"]
    in_specs = (
        P(None, "prow", None),
        P(None, "pcol", "prow"),
        P(None, "prow", "pcol"),
        P(None, "prow"),
    )
    out_specs = (P(None, "pcol", None), P(("prow", "pcol"), None))
    return jax.shard_map(
        functools.partial(per_device, chips, side, super_blocks),
        mesh=mesh, in_specs=in_specs, out_specs=out_specs, check_vma=False,
    )
```

```python
import functools
import math

import jax
import jax.numpy as jnp
from jax import lax
from jax.experimental import pallas as pl
from jax.experimental.pallas import tpu as pltpu
from jax.sharding import PartitionSpec as P

BLOCK_ROWS = 128
SUPER_BLOCKS = 32
SUPERNODES = 7
LEVELS = ((0, 4), (4, 2), (6, 1))
MESH = pl.DeviceIdType.MESH
F32 = jnp.float32
BF16 = jnp.bfloat16


def split(value):
    high = value.astype(BF16)
    low = (value - high.astype(F32)).astype(BF16)
    return high, low


def dot3(a_high, a_low, b_high, b_low):
    dot = functools.partial(jnp.dot, preferred_element_type=F32)
    width = b_high.shape[1]
    both = dot(a_high, jnp.concatenate([b_high, b_low], axis=1))
    return both[:, :width] + (both[:, width:] + dot(a_low, b_high))


def wait_bytes(ref, sem):
    pltpu.make_async_copy(ref, ref, sem).wait()


def kernel(
    chips, side, super_blocks, rows_ref, rhs_hbm, diag_hbm, panel_hbm, sol_hbm, up_hbm,
    rhs, diag, diag_high, diag_low, panel, panel_high, panel_low, terms, pair_in, half, ring_in, xs,
    prod, win, win_in, res, upper, up_in, up_mid, up_last, up_out,
    rhs_sem, diag_sem, panel_sem, pair_send, pair_recv, ring_send, ring_recv,
    gather_send, gather_recv, share_send, share_recv, win_send, win_recv, back_send, back_recv,
    up_send, up_recv, last_send, last_recv, out_sem,
):
    cols = side * side
    width = rhs.shape[3]
    prow = lax.axis_index("prow")
    pcol = lax.axis_index("pcol")
    chip, core = prow // 2, prow % 2
    col_x, col_y = pcol // side, pcol % side
    other = chip * 2 + 1 - core
    own_half, other_half = core * BLOCK_ROWS, (1 - core) * BLOCK_ROWS
    rows = BLOCK_ROWS // chips
    own_rows = own_half + chip * rows
    sent = []

    barrier = pltpu.get_barrier_semaphore()
    pl.semaphore_signal(barrier, inc=1, device_id=(other, pcol), device_id_type=MESH)

    def greet_chip(i, carry):
        peer = lax.rem(chip + i, chips) * 2 + core
        pl.semaphore_signal(barrier, inc=1, device_id=(peer, pcol), device_id_type=MESH)
        return carry

    def greet_col(i, carry):
        pl.semaphore_signal(
            barrier, inc=1, device_id=(prow, lax.rem(pcol + i, cols)), device_id_type=MESH
        )
        return carry

    lax.fori_loop(1, chips, greet_chip, 0)
    lax.fori_loop(1, cols, greet_col, 0)

    loads = {}
    for h in range(2):
        part = pl.ds(h * width, width)
        for level, (first, count) in enumerate(LEVELS):
            nodes = pl.ds(first, count)
            loads["rhs", h, level] = pltpu.make_async_copy(
                rhs_hbm.at[nodes, :, part], rhs.at[h, nodes], rhs_sem.at[h, level]
            )
    for k in range(SUPERNODES):
        loads["diag", k] = pltpu.make_async_copy(diag_hbm.at[k], diag.at[k], diag_sem.at[k])
        loads["panel", k] = pltpu.make_async_copy(panel_hbm.at[k], panel.at[k], panel_sem.at[k])
    loads["rhs", 0, 0].start()
    for k in range(4):
        loads["diag", k].start()
    loads["rhs", 1, 0].start()
    for k in range(4):
        loads["panel", k].start()
    for h in range(2):
        for level in (1, 2):
            loads["rhs", h, level].start()
    for k in range(4, SUPERNODES):
        loads["diag", k].start()
        loads["panel", k].start()

    def nodes_of(level):
        return pl.ds(*LEVELS[level])

    def each(level):
        first, count = LEVELS[level]
        return range(first, first + count)

    def split_diag(node):
        loads["diag", node].wait()
        diag_high[node], diag_low[node] = split(diag[node])

    def begin(level, h):
        for node in each(level):
            residual = rhs[h, node] if level == 0 else res[h, node - 4]
            r_high, r_low = split(residual)
            terms[h, node] = dot3(diag_high[node], diag_low[node], r_high, r_low)

    def pair(level, h):
        nodes = nodes_of(level)
        pltpu.make_async_remote_copy(
            src_ref=terms.at[h, nodes, pl.ds(other_half, BLOCK_ROWS)], dst_ref=pair_in.at[h, nodes],
            send_sem=pair_send.at[h, level], recv_sem=pair_recv.at[h, level],
            device_id=(other, pcol), device_id_type=MESH,
        ).start()
        sent.append((pair_in.at[h, nodes], pair_send.at[h, level]))

    def scatter(level, h):
        nodes = nodes_of(level)
        wait_bytes(pair_in.at[h, nodes], pair_recv.at[h, level])
        for node in each(level):
            half[h, node] = terms[h, node, pl.ds(own_half, BLOCK_ROWS)] + pair_in[h, node]

        def send(i, carry):
            peer = lax.rem(chip + i, chips)
            pltpu.make_async_remote_copy(
                src_ref=half.at[h, nodes, pl.ds(peer * rows, rows)], dst_ref=ring_in.at[h, i, nodes],
                send_sem=ring_send.at[h, level], recv_sem=ring_recv.at[h, level],
                device_id=(peer * 2 + core, pcol), device_id_type=MESH,
            ).start()
            return carry

        lax.fori_loop(1, chips, send, 0)
        sent.append((ring_in.at[h, pl.ds(1, chips - 1), nodes], ring_send.at[h, level]))

    def gather(level, h):
        nodes = nodes_of(level)
        wait_bytes(ring_in.at[h, pl.ds(1, chips - 1), nodes], ring_recv.at[h, level])
        for node in each(level):
            total = half[h, node, pl.ds(chip * rows, rows)]
            for i in range(1, chips):
                total = total + ring_in[h, i, node]
            xs[h, node, pl.ds(own_rows, rows)] = total
        here = xs.at[h, nodes, pl.ds(own_rows, rows)]

        def send(i, carry):
            peer = lax.rem(chip + i, chips)
            pltpu.make_async_remote_copy(
                src_ref=here, dst_ref=here,
                send_sem=gather_send.at[h, level], recv_sem=gather_recv.at[h, level],
                device_id=(peer * 2 + core, pcol), device_id_type=MESH,
            ).start()
            return carry

        lax.fori_loop(1, chips, send, 0)
        sent.append((ring_in.at[h, pl.ds(1, chips - 1), nodes], gather_send.at[h, level]))

    def share(level, h):
        nodes = nodes_of(level)
        wait_bytes(ring_in.at[h, pl.ds(1, chips - 1), nodes], gather_recv.at[h, level])
        here = xs.at[h, nodes, pl.ds(own_half, BLOCK_ROWS)]
        pltpu.make_async_remote_copy(
            src_ref=here, dst_ref=here,
            send_sem=share_send.at[h, level], recv_sem=share_recv.at[h, level],
            device_id=(other, pcol), device_id_type=MESH,
        ).start()
        sent.append((pair_in.at[h, nodes], share_send.at[h, level]))

    def multiply(level, h):
        wait_bytes(pair_in.at[h, nodes_of(level)], share_recv.at[h, level])
        for node in each(level):
            x_high, x_low = split(xs[h, node])
            product = dot3(panel_high[node], panel_low[node], x_high, x_low)
            for slot in range(8):
                prod[h, node, slot] = product[slot * BLOCK_ROWS:(slot + 1) * BLOCK_ROWS]

    def store(level, h):
        copy = pltpu.make_async_copy(
            xs.at[h, nodes_of(level)], sol_hbm.at[nodes_of(level), :, pl.ds(h * width, width)],
            out_sem.at[h, level],
        )
        copy.start()
        return copy

    def split_panel(node):
        loads["panel", node].wait()

        def one(step, carry):
            part = pl.ds(step * BLOCK_ROWS, BLOCK_ROWS)
            panel_high[node, part], panel_low[node, part] = split(panel[node, part])
            return carry

        lax.fori_loop(0, 8, one, 0)

    def picked(h, node, block):
        slot = 8
        for i in range(8):
            slot = jnp.where(rows_ref[node, i] == block, i, slot)
        return prod[h, node, slot]

    size = 2 * BLOCK_ROWS // cols
    windows = (pl.ds(0, 2), pl.ds(2, 1))
    targets = (((4, (0, 1)), (5, (2, 3))), ((6, (0, 1, 2, 3, 4, 5)),))

    def send_window(level, h):
        which = windows[level]
        for target, children in targets[level]:
            for b in range(2):
                block = target * super_blocks + prow * 2 + b
                total = picked(h, children[0], block)
                for node in children[1:]:
                    total = total + picked(h, node, block)
                win[h, target - 4, pl.ds(b * BLOCK_ROWS, BLOCK_ROWS)] = total

        def send(i, carry):
            peer = lax.rem(pcol + i, cols)
            pltpu.make_async_remote_copy(
                src_ref=win.at[h, which, pl.ds(peer * size, size)], dst_ref=win_in.at[h, i, which],
                send_sem=win_send.at[h, level], recv_sem=win_recv.at[h, level],
                device_id=(prow, peer), device_id_type=MESH,
            ).start()
            return carry

        lax.fori_loop(1, cols, send, 0)
        sent.append((win_in.at[h, pl.ds(1, cols - 1), which], win_send.at[h, level]))

    def spread(level, h):
        which = windows[level]
        loads["rhs", h, level + 1].wait()
        wait_bytes(win_in.at[h, pl.ds(1, cols - 1), which], win_recv.at[h, level])
        mine = pl.ds(pcol * size, size)
        for target, _ in targets[level]:
            total = win[h, target - 4, mine]
            for i in range(1, cols):
                total = total + win_in[h, i, target - 4]
            res[h, target - 4, mine] = rhs[h, target, mine] - total
        here = res.at[h, which, mine]

        def send(i, carry):
            pltpu.make_async_remote_copy(
                src_ref=here, dst_ref=here,
                send_sem=back_send.at[h, level], recv_sem=back_recv.at[h, level],
                device_id=(prow, lax.rem(pcol + i, cols)), device_id_type=MESH,
            ).start()
            return carry

        lax.fori_loop(1, cols, send, 0)
        sent.append((win_in.at[h, pl.ds(1, cols - 1), which], back_send.at[h, level]))

    def begin_next(level, h):
        wait_bytes(win_in.at[h, pl.ds(1, cols - 1), windows[level - 1]], back_recv.at[h, level - 1])
        begin(level, h)
        pair(level, h)

    def add_upper(which, h, nodes, fresh):
        count = upper.shape[4] // BLOCK_ROWS

        def one(j, carry):
            block = SUPERNODES * super_blocks + prow * 16 + j
            total = picked(h, nodes[0], block)
            for node in nodes[1:]:
                total = total + picked(h, node, block)
            place = j // count
            part = pl.ds((j % count) * BLOCK_ROWS, BLOCK_ROWS)
            spot = (which, h, place // side, place % side, part)
            upper[spot] = total if fresh else upper[spot] + total
            return carry

        lax.fori_loop(0, cols * count, one, 0)

    up_rows = upper.shape[4] // 2
    row_half = (pl.ds(0, up_rows), pl.ds(up_rows, up_rows))

    def send_upper(which, h):
        for i in range(1, side):
            peer_x, peer_y = lax.rem(col_x + i, side), lax.rem(col_y + i, side)
            pltpu.make_async_remote_copy(
                src_ref=upper.at[which, h, peer_x, :, row_half[0]], dst_ref=up_in.at[which, h, 0, i],
                send_sem=up_send.at[which, h, 0], recv_sem=up_recv.at[which, h, 0],
                device_id=(prow, peer_x * side + col_y), device_id_type=MESH,
            ).start()
            pltpu.make_async_remote_copy(
                src_ref=upper.at[which, h, :, peer_y, row_half[1]], dst_ref=up_in.at[which, h, 1, i],
                send_sem=up_send.at[which, h, 1], recv_sem=up_recv.at[which, h, 1],
                device_id=(prow, col_x * side + peer_y), device_id_type=MESH,
            ).start()
        for way in range(2):
            sent.append((up_in.at[which, h, way, pl.ds(1, side - 1)], up_send.at[which, h, way]))

    def middle_upper(which, h):
        for way in range(2):
            wait_bytes(up_in.at[which, h, way, pl.ds(1, side - 1)], up_recv.at[which, h, way])

            def one(j, carry):
                if way == 0:
                    total = upper[which, h, col_x, j, row_half[0]]
                else:
                    total = upper[which, h, j, col_y, row_half[1]]
                for i in range(1, side):
                    total = total + up_in[which, h, way, i, j]
                up_mid[which, h, way, j] = total
                return carry

            lax.fori_loop(0, side, one, 0)
            for i in range(1, side):
                if way == 0:
                    place = lax.rem(col_y + i, side)
                    peer = col_x * side + place
                else:
                    place = lax.rem(col_x + i, side)
                    peer = place * side + col_y
                pltpu.make_async_remote_copy(
                    src_ref=up_mid.at[which, h, way, place], dst_ref=up_last.at[which, h, way, i],
                    send_sem=last_send.at[which, h, way], recv_sem=last_recv.at[which, h, way],
                    device_id=(prow, peer), device_id_type=MESH,
                ).start()
            sent.append((up_last.at[which, h, way, pl.ds(1, side - 1)], last_send.at[which, h, way]))

    def finish_upper(which, h, fresh):
        for way in range(2):
            wait_bytes(up_last.at[which, h, way, pl.ds(1, side - 1)], last_recv.at[which, h, way])
            total = up_mid[which, h, way, col_y if way == 0 else col_x]
            for i in range(1, side):
                total = total + up_last[which, h, way, i]
            goal = (row_half[way], pl.ds(h * width, width))
            up_out[goal] = total if fresh else up_out[goal] + total

    def drain(count):
        for ref, sem in sent[:count]:
            wait_bytes(ref, sem)
        del sent[:count]

    def run():
        stores = []
        for h in range(2):
            loads["rhs", h, 0].wait()
            if h == 0:
                for node in range(4):
                    split_diag(node)
            begin(0, h)
        pl.semaphore_wait(barrier, chips + cols - 1)
        for h in range(2):
            pair(0, h)
        yield
        for h in range(2):
            scatter(0, h)
        for h in range(2):
            for node in range(SUPERNODES):
                prod[h, node, 8] = jnp.zeros((BLOCK_ROWS, width), F32)
        for node in range(SUPERNODES):
            split_panel(node)
        for node in range(4, SUPERNODES):
            split_diag(node)
        yield
        for h in range(2):
            gather(0, h)
        yield
        for h in range(2):
            share(0, h)
            multiply(0, h)
            send_window(0, h)
        yield
        for h in range(2):
            spread(0, h)
        yield
        for h in range(2):
            stores.append(store(0, h))
            add_upper(0, h, (0, 1, 2, 3), True)
        for h in range(2):
            begin_next(1, h)
        yield
        for h in range(2):
            scatter(1, h)
        for h in range(2):
            send_upper(0, h)
        for h in range(2):
            gather(1, h)
        yield
        share(1, 0)
        multiply(1, 0)
        share(1, 1)
        send_window(1, 0)
        multiply(1, 1)
        send_window(1, 1)
        yield
        for h in range(2):
            stores.append(store(1, h))
            add_upper(1, h, (4, 5), True)
        for h in range(2):
            spread(1, h)
        yield
        for h in range(2):
            begin_next(2, h)
        for h in range(2):
            scatter(2, h)
        for h in range(2):
            middle_upper(0, h)
        for h in range(2):
            gather(2, h)
        yield
        for h in range(2):
            share(2, h)
        early = len(sent)
        for h in range(2):
            multiply(2, h)
            add_upper(1, h, (6,), False)
            send_upper(1, h)
        yield
        for h in range(2):
            stores.append(store(2, h))
            finish_upper(0, h, True)
        drain(early)
        for copy in stores:
            copy.wait()
        for h in range(2):
            middle_upper(1, h)
        for h in range(2):
            finish_upper(1, h, False)
        last = pltpu.make_async_copy(up_out, up_hbm, out_sem.at[0, 3])
        last.start()
        drain(len(sent))
        last.wait()

    for _ in run():
        pass


def copy_out(sol_ref, up_ref, sol_out, up_out, sems):
    copies = [
        pltpu.make_async_copy(sol_ref.at[k], sol_out.at[k], sems.at[k]) for k in range(SUPERNODES)
    ]
    copies.append(pltpu.make_async_copy(up_ref, up_out, sems.at[SUPERNODES]))
    for copy in copies:
        copy.start()
    for copy in copies:
        copy.wait()


def per_device(chips, side, super_blocks, right_side, inverse_diag, panels, block_rows):
    rhs_cols = right_side.shape[2]
    order = right_side.shape[1]
    upper_own = 2 * block_rows.shape[1]
    rows = BLOCK_ROWS // chips
    cols = side * side
    own_upper = upper_own * BLOCK_ROWS // cols
    dma = pltpu.SemaphoreType.DMA
    width = rhs_cols // 2
    scratch = [
        pltpu.VMEM((2, 7, order, width), F32),
        pltpu.VMEM((7, order, order), F32),
        pltpu.VMEM((7, order, order), BF16),
        pltpu.VMEM((7, order, order), BF16),
        pltpu.VMEM(panels.shape, F32),
        pltpu.VMEM(panels.shape, BF16),
        pltpu.VMEM(panels.shape, BF16),
        pltpu.VMEM((2, 7, order, width), F32),
        pltpu.VMEM((2, 7, BLOCK_ROWS, width), F32),
        pltpu.VMEM((2, 7, BLOCK_ROWS, width), F32),
        pltpu.VMEM((2, chips, 7, rows, width), F32),
        pltpu.VMEM((2, 7, order, width), F32),
        pltpu.VMEM((2, 7, 9, BLOCK_ROWS, width), F32),
        pltpu.VMEM((2, 3, order, width), F32),
        pltpu.VMEM((2, cols, 3, order // cols, width), F32),
        pltpu.VMEM((2, 3, order, width), F32),
        pltpu.VMEM((2, 2, side, side, own_upper, width), F32),
        pltpu.VMEM((2, 2, 2, side, side, own_upper // 2, width), F32),
        pltpu.VMEM((2, 2, 2, side, own_upper // 2, width), F32),
        pltpu.VMEM((2, 2, 2, side, own_upper // 2, width), F32),
        pltpu.VMEM((own_upper, rhs_cols), F32),
        dma((2, 3)), dma((7,)), dma((7,)), dma((2, 3)), dma((2, 3)), dma((2, 3)), dma((2, 3)),
        dma((2, 3)), dma((2, 3)), dma((2, 3)), dma((2, 3)), dma((2, 2)), dma((2, 2)), dma((2, 2)), dma((2, 2)),
        dma((2, 2, 2)), dma((2, 2, 2)), dma((2, 2, 2)), dma((2, 2, 2)), dma((2, 4)),
    ]
    anywhere = pl.BlockSpec(memory_space=pl.ANY)
    stay = pl.BlockSpec(memory_space=pltpu.HBM)
    shapes = (
        jax.ShapeDtypeStruct((7, order, rhs_cols), F32),
        jax.ShapeDtypeStruct((own_upper, rhs_cols), F32),
    )
    results = pl.pallas_call(
        functools.partial(kernel, chips, side, super_blocks),
        out_shape=shapes,
        in_specs=[pl.BlockSpec(memory_space=pltpu.SMEM), stay, stay, stay],
        out_specs=(anywhere, anywhere),
        scratch_shapes=scratch,
        compiler_params=pltpu.CompilerParams(
            collective_id=0, has_side_effects=True, vmem_limit_bytes=52 * 1024 * 1024
        ),
    )(block_rows, right_side, inverse_diag, panels)
    return pl.pallas_call(
        copy_out,
        out_shape=shapes,
        in_specs=[pl.BlockSpec(memory_space=pltpu.VMEM)] * 2,
        out_specs=(stay, stay),
        scratch_shapes=[dma((8,))],
        compiler_params=pltpu.CompilerParams(vmem_limit_bytes=8 * 1024 * 1024),
    )(*results)


def solution(mesh):
    chips, side = mesh.shape["prow"] // 2, math.isqrt(mesh.shape["pcol"])
    super_blocks = 2 * mesh.shape["prow"]
    in_specs = (
        P(None, "prow", None),
        P(None, "pcol", "prow"),
        P(None, "prow", "pcol"),
        P(None, "prow"),
    )
    out_specs = (P(None, "pcol", None), P(("prow", "pcol"), None))
    return jax.shard_map(
        functools.partial(per_device, chips, side, super_blocks),
        mesh=mesh, in_specs=in_specs, out_specs=out_specs, check_vma=False,
    )
```

```python
import functools
import math

import jax
import jax.numpy as jnp
from jax import lax
from jax.experimental import pallas as pl
from jax.experimental.pallas import tpu as pltpu
from jax.sharding import PartitionSpec as P

BLOCK_ROWS = 128
SUPER_BLOCKS = 32
SUPERNODES = 7
LEVELS = ((0, 4), (4, 2), (6, 1))
MESH = pl.DeviceIdType.MESH
F32 = jnp.float32
BF16 = jnp.bfloat16


def split(value):
    high = value.astype(BF16)
    low = (value - high.astype(F32)).astype(BF16)
    return high, low


def dot3(a_high, a_low, b_high, b_low):
    dot = functools.partial(jnp.dot, preferred_element_type=F32)
    width = b_high.shape[1]
    both = dot(a_high, jnp.concatenate([b_high, b_low], axis=1))
    return both[:, :width] + (both[:, width:] + dot(a_low, b_high))


def wait_bytes(ref, sem):
    pltpu.make_async_copy(ref, ref, sem).wait()


def kernel(
    chips, side, super_blocks, rows_ref, rhs_hbm, diag_hbm, panel_hbm, sol_hbm, up_hbm,
    rhs, diag, diag_high, diag_low, panel, panel_high, panel_low, terms, pair_in, half, ring_in, xs,
    prod, win, win_in, res, upper, up_in, up_mid, up_last, up_out,
    rhs_sem, diag_sem, panel_sem, pair_send, pair_recv, ring_send, ring_recv,
    gather_send, gather_recv, share_send, share_recv, win_send, win_recv, back_send, back_recv,
    up_send, up_recv, last_send, last_recv, out_sem,
):
    cols = side * side
    width = rhs.shape[3]
    prow = lax.axis_index("prow")
    pcol = lax.axis_index("pcol")
    chip, core = prow // 2, prow % 2
    col_x, col_y = pcol // side, pcol % side
    other = chip * 2 + 1 - core
    own_half, other_half = core * BLOCK_ROWS, (1 - core) * BLOCK_ROWS
    rows = BLOCK_ROWS // chips
    own_rows = own_half + chip * rows
    sent = []

    barrier = pltpu.get_barrier_semaphore()
    pl.semaphore_signal(barrier, inc=1, device_id=(other, pcol), device_id_type=MESH)

    def greet_chip(i, carry):
        peer = lax.rem(chip + i, chips) * 2 + core
        pl.semaphore_signal(barrier, inc=1, device_id=(peer, pcol), device_id_type=MESH)
        return carry

    def greet_col(i, carry):
        pl.semaphore_signal(
            barrier, inc=1, device_id=(prow, lax.rem(pcol + i, cols)), device_id_type=MESH
        )
        return carry

    lax.fori_loop(1, chips, greet_chip, 0)
    lax.fori_loop(1, cols, greet_col, 0)

    loads = {}
    for h in range(2):
        part = pl.ds(h * width, width)
        for level, (first, count) in enumerate(LEVELS):
            nodes = pl.ds(first, count)
            loads["rhs", h, level] = pltpu.make_async_copy(
                rhs_hbm.at[nodes, :, part], rhs.at[h, nodes], rhs_sem.at[h, level]
            )
    for k in range(SUPERNODES):
        loads["diag", k] = pltpu.make_async_copy(diag_hbm.at[k], diag.at[k], diag_sem.at[k])
        loads["panel", k] = pltpu.make_async_copy(panel_hbm.at[k], panel.at[k], panel_sem.at[k])
    loads["rhs", 0, 0].start()
    for k in range(4):
        loads["diag", k].start()
    loads["rhs", 1, 0].start()
    for k in range(4):
        loads["panel", k].start()
    for h in range(2):
        for level in (1, 2):
            loads["rhs", h, level].start()
    for k in range(4, SUPERNODES):
        loads["diag", k].start()
        loads["panel", k].start()

    def hops(i, count):
        return min(i, count - i)

    far_chips = sorted(range(1, chips), key=lambda i: -hops(i, chips))
    far_cols = sorted(
        range(1, cols), key=lambda i: -hops(i // side, side) - hops(i % side, side)
    )

    def col_peer(i):
        return lax.rem(col_x + i // side, side) * side + lax.rem(col_y + i % side, side)

    def to_chips(send):
        for i in far_chips:
            send(i, 0)

    def to_cols(send):
        for i in far_cols:
            send(i, 0)

    def nodes_of(level):
        return pl.ds(*LEVELS[level])

    def each(level):
        first, count = LEVELS[level]
        return range(first, first + count)

    def split_diag(node):
        loads["diag", node].wait()
        diag_high[node], diag_low[node] = split(diag[node])

    def begin(level, h):
        for node in each(level):
            residual = rhs[h, node] if level == 0 else res[h, node - 4]
            r_high, r_low = split(residual)
            terms[h, node] = dot3(diag_high[node], diag_low[node], r_high, r_low)

    def pair(level, h):
        nodes = nodes_of(level)
        pltpu.make_async_remote_copy(
            src_ref=terms.at[h, nodes, pl.ds(other_half, BLOCK_ROWS)], dst_ref=pair_in.at[h, nodes],
            send_sem=pair_send.at[h, level], recv_sem=pair_recv.at[h, level],
            device_id=(other, pcol), device_id_type=MESH,
        ).start()
        sent.append((pair_in.at[h, nodes], pair_send.at[h, level]))

    def scatter(level, h):
        nodes = nodes_of(level)
        wait_bytes(pair_in.at[h, nodes], pair_recv.at[h, level])
        for node in each(level):
            half[h, node] = terms[h, node, pl.ds(own_half, BLOCK_ROWS)] + pair_in[h, node]

        def send(i, carry):
            peer = lax.rem(chip + i, chips)
            pltpu.make_async_remote_copy(
                src_ref=half.at[h, nodes, pl.ds(peer * rows, rows)], dst_ref=ring_in.at[h, i, nodes],
                send_sem=ring_send.at[h, level], recv_sem=ring_recv.at[h, level],
                device_id=(peer * 2 + core, pcol), device_id_type=MESH,
            ).start()
            return carry

        to_chips(send)
        sent.append((ring_in.at[h, pl.ds(1, chips - 1), nodes], ring_send.at[h, level]))

    def gather(level, h):
        nodes = nodes_of(level)
        wait_bytes(ring_in.at[h, pl.ds(1, chips - 1), nodes], ring_recv.at[h, level])
        for node in each(level):
            total = half[h, node, pl.ds(chip * rows, rows)]
            for i in range(1, chips):
                total = total + ring_in[h, i, node]
            xs[h, node, pl.ds(own_rows, rows)] = total
        here = xs.at[h, nodes, pl.ds(own_rows, rows)]

        def send(i, carry):
            peer = lax.rem(chip + i, chips)
            pltpu.make_async_remote_copy(
                src_ref=here, dst_ref=here,
                send_sem=gather_send.at[h, level], recv_sem=gather_recv.at[h, level],
                device_id=(peer * 2 + core, pcol), device_id_type=MESH,
            ).start()
            return carry

        to_chips(send)
        sent.append((ring_in.at[h, pl.ds(1, chips - 1), nodes], gather_send.at[h, level]))

    def share(level, h):
        nodes = nodes_of(level)
        wait_bytes(ring_in.at[h, pl.ds(1, chips - 1), nodes], gather_recv.at[h, level])
        here = xs.at[h, nodes, pl.ds(own_half, BLOCK_ROWS)]
        pltpu.make_async_remote_copy(
            src_ref=here, dst_ref=here,
            send_sem=share_send.at[h, level], recv_sem=share_recv.at[h, level],
            device_id=(other, pcol), device_id_type=MESH,
        ).start()
        sent.append((pair_in.at[h, nodes], share_send.at[h, level]))

    def multiply(level, h):
        wait_bytes(pair_in.at[h, nodes_of(level)], share_recv.at[h, level])
        for node in each(level):
            x_high, x_low = split(xs[h, node])
            product = dot3(panel_high[node], panel_low[node], x_high, x_low)
            for slot in range(8):
                prod[h, node, slot] = product[slot * BLOCK_ROWS:(slot + 1) * BLOCK_ROWS]

    def store(level, h):
        copy = pltpu.make_async_copy(
            xs.at[h, nodes_of(level)], sol_hbm.at[nodes_of(level), :, pl.ds(h * width, width)],
            out_sem.at[h, level],
        )
        copy.start()
        return copy

    def split_panel(node):
        loads["panel", node].wait()

        def one(step, carry):
            part = pl.ds(step * BLOCK_ROWS, BLOCK_ROWS)
            panel_high[node, part], panel_low[node, part] = split(panel[node, part])
            return carry

        lax.fori_loop(0, 8, one, 0)

    def picked(h, node, block):
        slot = 8
        for i in range(8):
            slot = jnp.where(rows_ref[node, i] == block, i, slot)
        return prod[h, node, slot]

    size = 2 * BLOCK_ROWS // cols
    windows = (pl.ds(0, 2), pl.ds(2, 1))
    targets = (((4, (0, 1)), (5, (2, 3))), ((6, (0, 1, 2, 3, 4, 5)),))

    def send_window(level, h):
        which = windows[level]
        for target, children in targets[level]:
            for b in range(2):
                block = target * super_blocks + prow * 2 + b
                total = picked(h, children[0], block)
                for node in children[1:]:
                    total = total + picked(h, node, block)
                win[h, target - 4, pl.ds(b * BLOCK_ROWS, BLOCK_ROWS)] = total

        def send(i, carry):
            peer = col_peer(i)
            pltpu.make_async_remote_copy(
                src_ref=win.at[h, which, pl.ds(peer * size, size)], dst_ref=win_in.at[h, i, which],
                send_sem=win_send.at[h, level], recv_sem=win_recv.at[h, level],
                device_id=(prow, peer), device_id_type=MESH,
            ).start()
            return carry

        to_cols(send)
        sent.append((win_in.at[h, pl.ds(1, cols - 1), which], win_send.at[h, level]))

    def spread(level, h):
        which = windows[level]
        loads["rhs", h, level + 1].wait()
        wait_bytes(win_in.at[h, pl.ds(1, cols - 1), which], win_recv.at[h, level])
        mine = pl.ds(pcol * size, size)
        for target, _ in targets[level]:
            total = win[h, target - 4, mine]
            for i in range(1, cols):
                total = total + win_in[h, i, target - 4]
            res[h, target - 4, mine] = rhs[h, target, mine] - total
        here = res.at[h, which, mine]

        def send(i, carry):
            pltpu.make_async_remote_copy(
                src_ref=here, dst_ref=here,
                send_sem=back_send.at[h, level], recv_sem=back_recv.at[h, level],
                device_id=(prow, col_peer(i)), device_id_type=MESH,
            ).start()
            return carry

        to_cols(send)
        sent.append((win_in.at[h, pl.ds(1, cols - 1), which], back_send.at[h, level]))

    def begin_next(level, h):
        wait_bytes(win_in.at[h, pl.ds(1, cols - 1), windows[level - 1]], back_recv.at[h, level - 1])
        begin(level, h)
        pair(level, h)

    def add_upper(which, h, nodes, fresh):
        count = upper.shape[4] // BLOCK_ROWS

        def one(j, carry):
            block = SUPERNODES * super_blocks + prow * 16 + j
            total = picked(h, nodes[0], block)
            for node in nodes[1:]:
                total = total + picked(h, node, block)
            place = j // count
            part = pl.ds((j % count) * BLOCK_ROWS, BLOCK_ROWS)
            spot = (which, h, place // side, place % side, part)
            upper[spot] = total if fresh else upper[spot] + total
            return carry

        lax.fori_loop(0, cols * count, one, 0)

    up_rows = upper.shape[4] // 2
    row_half = (pl.ds(0, up_rows), pl.ds(up_rows, up_rows))

    def send_upper(which, h):
        for i in range(1, side):
            peer_x, peer_y = lax.rem(col_x + i, side), lax.rem(col_y + i, side)
            pltpu.make_async_remote_copy(
                src_ref=upper.at[which, h, peer_x, :, row_half[0]], dst_ref=up_in.at[which, h, 0, i],
                send_sem=up_send.at[which, h, 0], recv_sem=up_recv.at[which, h, 0],
                device_id=(prow, peer_x * side + col_y), device_id_type=MESH,
            ).start()
            pltpu.make_async_remote_copy(
                src_ref=upper.at[which, h, :, peer_y, row_half[1]], dst_ref=up_in.at[which, h, 1, i],
                send_sem=up_send.at[which, h, 1], recv_sem=up_recv.at[which, h, 1],
                device_id=(prow, col_x * side + peer_y), device_id_type=MESH,
            ).start()
        for way in range(2):
            sent.append((up_in.at[which, h, way, pl.ds(1, side - 1)], up_send.at[which, h, way]))

    def middle_upper(which, h):
        for way in range(2):
            wait_bytes(up_in.at[which, h, way, pl.ds(1, side - 1)], up_recv.at[which, h, way])

            def one(j, carry):
                if way == 0:
                    total = upper[which, h, col_x, j, row_half[0]]
                else:
                    total = upper[which, h, j, col_y, row_half[1]]
                for i in range(1, side):
                    total = total + up_in[which, h, way, i, j]
                up_mid[which, h, way, j] = total
                return carry

            lax.fori_loop(0, side, one, 0)
            for i in range(1, side):
                if way == 0:
                    place = lax.rem(col_y + i, side)
                    peer = col_x * side + place
                else:
                    place = lax.rem(col_x + i, side)
                    peer = place * side + col_y
                pltpu.make_async_remote_copy(
                    src_ref=up_mid.at[which, h, way, place], dst_ref=up_last.at[which, h, way, i],
                    send_sem=last_send.at[which, h, way], recv_sem=last_recv.at[which, h, way],
                    device_id=(prow, peer), device_id_type=MESH,
                ).start()
            sent.append((up_last.at[which, h, way, pl.ds(1, side - 1)], last_send.at[which, h, way]))

    def finish_upper(which, h, fresh):
        for way in range(2):
            wait_bytes(up_last.at[which, h, way, pl.ds(1, side - 1)], last_recv.at[which, h, way])
            total = up_mid[which, h, way, col_y if way == 0 else col_x]
            for i in range(1, side):
                total = total + up_last[which, h, way, i]
            goal = (row_half[way], pl.ds(h * width, width))
            up_out[goal] = total if fresh else up_out[goal] + total

    def drain(count):
        for ref, sem in sent[:count]:
            wait_bytes(ref, sem)
        del sent[:count]

    def run():
        stores = []
        for h in range(2):
            loads["rhs", h, 0].wait()
            if h == 0:
                for node in range(4):
                    split_diag(node)
            begin(0, h)
        pl.semaphore_wait(barrier, chips + cols - 1)
        for h in range(2):
            pair(0, h)
        yield
        for h in range(2):
            scatter(0, h)
        for h in range(2):
            for node in range(SUPERNODES):
                prod[h, node, 8] = jnp.zeros((BLOCK_ROWS, width), F32)
        for node in range(SUPERNODES):
            split_panel(node)
        for node in range(4, SUPERNODES):
            split_diag(node)
        yield
        for h in range(2):
            gather(0, h)
        yield
        for h in range(2):
            share(0, h)
            multiply(0, h)
            send_window(0, h)
        yield
        for h in range(2):
            spread(0, h)
        yield
        for h in range(2):
            stores.append(store(0, h))
            add_upper(0, h, (0, 1, 2, 3), True)
        for h in range(2):
            begin_next(1, h)
        yield
        for h in range(2):
            scatter(1, h)
        for h in range(2):
            send_upper(0, h)
        for h in range(2):
            gather(1, h)
        yield
        share(1, 0)
        multiply(1, 0)
        share(1, 1)
        send_window(1, 0)
        multiply(1, 1)
        send_window(1, 1)
        yield
        for h in range(2):
            stores.append(store(1, h))
            add_upper(1, h, (4, 5), True)
        for h in range(2):
            spread(1, h)
        yield
        for h in range(2):
            begin_next(2, h)
        for h in range(2):
            scatter(2, h)
        for h in range(2):
            middle_upper(0, h)
        for h in range(2):
            gather(2, h)
        yield
        for h in range(2):
            share(2, h)
        early = len(sent)
        for h in range(2):
            multiply(2, h)
            add_upper(1, h, (6,), False)
            send_upper(1, h)
        yield
        for h in range(2):
            stores.append(store(2, h))
            finish_upper(0, h, True)
        drain(early)
        for copy in stores:
            copy.wait()
        for h in range(2):
            middle_upper(1, h)
        for h in range(2):
            finish_upper(1, h, False)
        last = pltpu.make_async_copy(up_out, up_hbm, out_sem.at[0, 3])
        last.start()
        drain(len(sent))
        last.wait()

    for _ in run():
        pass


def copy_out(sol_ref, up_ref, sol_out, up_out, sems):
    copies = [
        pltpu.make_async_copy(sol_ref.at[k], sol_out.at[k], sems.at[k]) for k in range(SUPERNODES)
    ]
    copies.append(pltpu.make_async_copy(up_ref, up_out, sems.at[SUPERNODES]))
    for copy in copies:
        copy.start()
    for copy in copies:
        copy.wait()


def per_device(chips, side, super_blocks, right_side, inverse_diag, panels, block_rows):
    rhs_cols = right_side.shape[2]
    order = right_side.shape[1]
    upper_own = 2 * block_rows.shape[1]
    rows = BLOCK_ROWS // chips
    cols = side * side
    own_upper = upper_own * BLOCK_ROWS // cols
    dma = pltpu.SemaphoreType.DMA
    width = rhs_cols // 2
    scratch = [
        pltpu.VMEM((2, 7, order, width), F32),
        pltpu.VMEM((7, order, order), F32),
        pltpu.VMEM((7, order, order), BF16),
        pltpu.VMEM((7, order, order), BF16),
        pltpu.VMEM(panels.shape, F32),
        pltpu.VMEM(panels.shape, BF16),
        pltpu.VMEM(panels.shape, BF16),
        pltpu.VMEM((2, 7, order, width), F32),
        pltpu.VMEM((2, 7, BLOCK_ROWS, width), F32),
        pltpu.VMEM((2, 7, BLOCK_ROWS, width), F32),
        pltpu.VMEM((2, chips, 7, rows, width), F32),
        pltpu.VMEM((2, 7, order, width), F32),
        pltpu.VMEM((2, 7, 9, BLOCK_ROWS, width), F32),
        pltpu.VMEM((2, 3, order, width), F32),
        pltpu.VMEM((2, cols, 3, order // cols, width), F32),
        pltpu.VMEM((2, 3, order, width), F32),
        pltpu.VMEM((2, 2, side, side, own_upper, width), F32),
        pltpu.VMEM((2, 2, 2, side, side, own_upper // 2, width), F32),
        pltpu.VMEM((2, 2, 2, side, own_upper // 2, width), F32),
        pltpu.VMEM((2, 2, 2, side, own_upper // 2, width), F32),
        pltpu.VMEM((own_upper, rhs_cols), F32),
        dma((2, 3)), dma((7,)), dma((7,)), dma((2, 3)), dma((2, 3)), dma((2, 3)), dma((2, 3)),
        dma((2, 3)), dma((2, 3)), dma((2, 3)), dma((2, 3)), dma((2, 2)), dma((2, 2)), dma((2, 2)), dma((2, 2)),
        dma((2, 2, 2)), dma((2, 2, 2)), dma((2, 2, 2)), dma((2, 2, 2)), dma((2, 4)),
    ]
    anywhere = pl.BlockSpec(memory_space=pl.ANY)
    stay = pl.BlockSpec(memory_space=pltpu.HBM)
    shapes = (
        jax.ShapeDtypeStruct((7, order, rhs_cols), F32),
        jax.ShapeDtypeStruct((own_upper, rhs_cols), F32),
    )
    results = pl.pallas_call(
        functools.partial(kernel, chips, side, super_blocks),
        out_shape=shapes,
        in_specs=[pl.BlockSpec(memory_space=pltpu.SMEM), stay, stay, stay],
        out_specs=(anywhere, anywhere),
        scratch_shapes=scratch,
        compiler_params=pltpu.CompilerParams(
            collective_id=0, has_side_effects=True, vmem_limit_bytes=52 * 1024 * 1024
        ),
    )(block_rows, right_side, inverse_diag, panels)
    return pl.pallas_call(
        copy_out,
        out_shape=shapes,
        in_specs=[pl.BlockSpec(memory_space=pltpu.VMEM)] * 2,
        out_specs=(stay, stay),
        scratch_shapes=[dma((8,))],
        compiler_params=pltpu.CompilerParams(vmem_limit_bytes=8 * 1024 * 1024),
    )(*results)


def solution(mesh):
    chips, side = mesh.shape["prow"] // 2, math.isqrt(mesh.shape["pcol"])
    super_blocks = 2 * mesh.shape["prow"]
    in_specs = (
        P(None, "prow", None),
        P(None, "pcol", "prow"),
        P(None, "prow", "pcol"),
        P(None, "prow"),
    )
    out_specs = (P(None, "pcol", None), P(("prow", "pcol"), None))
    return jax.shard_map(
        functools.partial(per_device, chips, side, super_blocks),
        mesh=mesh, in_specs=in_specs, out_specs=out_specs, check_vma=False,
    )
```

```python
import functools
import math

import jax
import jax.numpy as jnp
from jax import lax
from jax.experimental import pallas as pl
from jax.experimental.pallas import tpu as pltpu
from jax.sharding import PartitionSpec as P

BLOCK_ROWS = 128
SUPER_BLOCKS = 32
SUPERNODES = 7
LEVELS = ((0, 4), (4, 2), (6, 1))
MESH = pl.DeviceIdType.MESH
F32 = jnp.float32
BF16 = jnp.bfloat16


def split(value):
    high = value.astype(BF16)
    low = (value - high.astype(F32)).astype(BF16)
    return high, low


def dot3(a_high, a_low, b_high, b_low):
    dot = functools.partial(jnp.dot, preferred_element_type=F32)
    width = b_high.shape[1]
    both = dot(a_high, jnp.concatenate([b_high, b_low], axis=1))
    return both[:, :width] + (both[:, width:] + dot(a_low, b_high))


def wait_bytes(ref, sem):
    pltpu.make_async_copy(ref, ref, sem).wait()


def kernel(
    chips, side, super_blocks, rows_ref, rhs_hbm, diag_hbm, panel_hbm, sol_hbm, up_hbm,
    rhs, diag, diag_high, diag_low, panel, panel_high, panel_low, terms, pair_in, half, ring_in, xs,
    prod, win, win_in, res, upper, up_in, up_mid, up_last, up_out,
    rhs_sem, diag_sem, panel_sem, pair_send, pair_recv, ring_send, ring_recv,
    gather_send, gather_recv, share_send, share_recv, win_send, win_recv, back_send, back_recv,
    up_send, up_recv, last_send, last_recv, out_sem,
):
    cols = side * side
    width = rhs.shape[3]
    prow = lax.axis_index("prow")
    pcol = lax.axis_index("pcol")
    chip, core = prow // 2, prow % 2
    col_x, col_y = pcol // side, pcol % side
    other = chip * 2 + 1 - core
    own_half, other_half = core * BLOCK_ROWS, (1 - core) * BLOCK_ROWS
    rows = BLOCK_ROWS // chips
    own_rows = own_half + chip * rows
    sent = []

    barrier = pltpu.get_barrier_semaphore()
    pl.semaphore_signal(barrier, inc=1, device_id=(other, pcol), device_id_type=MESH)

    def greet_chip(i, carry):
        peer = lax.rem(chip + i, chips) * 2 + core
        pl.semaphore_signal(barrier, inc=1, device_id=(peer, pcol), device_id_type=MESH)
        return carry

    def greet_col(i, carry):
        pl.semaphore_signal(
            barrier, inc=1, device_id=(prow, lax.rem(pcol + i, cols)), device_id_type=MESH
        )
        return carry

    lax.fori_loop(1, chips, greet_chip, 0)
    lax.fori_loop(1, cols, greet_col, 0)

    loads = {}
    for h in range(2):
        part = pl.ds(h * width, width)
        for level, (first, count) in enumerate(LEVELS):
            nodes = pl.ds(first, count)
            loads["rhs", h, level] = pltpu.make_async_copy(
                rhs_hbm.at[nodes, :, part], rhs.at[h, nodes], rhs_sem.at[h, level]
            )
    for k in range(SUPERNODES):
        loads["diag", k] = pltpu.make_async_copy(diag_hbm.at[k], diag.at[k], diag_sem.at[k])
        loads["panel", k] = pltpu.make_async_copy(panel_hbm.at[k], panel.at[k], panel_sem.at[k])
    loads["rhs", 0, 0].start()
    for k in range(4):
        loads["diag", k].start()
    loads["rhs", 1, 0].start()
    for k in range(4):
        loads["panel", k].start()
    for h in range(2):
        for level in (1, 2):
            loads["rhs", h, level].start()
    for k in range(4, SUPERNODES):
        loads["diag", k].start()
        loads["panel", k].start()

    def hops(i, count):
        return min(i, count - i)

    far_chips = sorted(range(1, chips), key=lambda i: -hops(i, chips))
    far_cols = sorted(
        range(1, cols), key=lambda i: -hops(i // side, side) - hops(i % side, side)
    )

    def col_peer(i):
        return lax.rem(col_x + i // side, side) * side + lax.rem(col_y + i % side, side)

    def to_chips(send):
        for i in far_chips:
            send(i, 0)

    def to_cols(send):
        for i in far_cols:
            send(i, 0)

    def nodes_of(level):
        return pl.ds(*LEVELS[level])

    def each(level):
        first, count = LEVELS[level]
        return range(first, first + count)

    def split_diag(node):
        loads["diag", node].wait()
        diag_high[node], diag_low[node] = split(diag[node])

    def begin(level, h):
        for node in each(level):
            residual = rhs[h, node] if level == 0 else res[h, node - 4]
            r_high, r_low = split(residual)
            terms[h, node] = dot3(diag_high[node], diag_low[node], r_high, r_low)

    def pair(level, h):
        nodes = nodes_of(level)
        pltpu.make_async_remote_copy(
            src_ref=terms.at[h, nodes, pl.ds(other_half, BLOCK_ROWS)], dst_ref=pair_in.at[h, nodes],
            send_sem=pair_send.at[h, level], recv_sem=pair_recv.at[h, level],
            device_id=(other, pcol), device_id_type=MESH,
        ).start()
        sent.append((pair_in.at[h, nodes], pair_send.at[h, level]))

    def scatter(level, h):
        nodes = nodes_of(level)
        wait_bytes(pair_in.at[h, nodes], pair_recv.at[h, level])
        for node in each(level):
            half[h, node] = terms[h, node, pl.ds(own_half, BLOCK_ROWS)] + pair_in[h, node]

        def send(i, carry):
            peer = lax.rem(chip + i, chips)
            pltpu.make_async_remote_copy(
                src_ref=half.at[h, nodes, pl.ds(peer * rows, rows)], dst_ref=ring_in.at[h, i, nodes],
                send_sem=ring_send.at[h, level], recv_sem=ring_recv.at[h, level],
                device_id=(peer * 2 + core, pcol), device_id_type=MESH,
            ).start()
            return carry

        to_chips(send)
        sent.append((ring_in.at[h, pl.ds(1, chips - 1), nodes], ring_send.at[h, level]))

    def gather(level, h):
        nodes = nodes_of(level)
        wait_bytes(ring_in.at[h, pl.ds(1, chips - 1), nodes], ring_recv.at[h, level])
        for node in each(level):
            total = half[h, node, pl.ds(chip * rows, rows)]
            for i in range(1, chips):
                total = total + ring_in[h, i, node]
            xs[h, node, pl.ds(own_rows, rows)] = total
        here = xs.at[h, nodes, pl.ds(own_rows, rows)]

        def send(i, carry):
            peer = lax.rem(chip + i, chips)
            pltpu.make_async_remote_copy(
                src_ref=here, dst_ref=here,
                send_sem=gather_send.at[h, level], recv_sem=gather_recv.at[h, level],
                device_id=(peer * 2 + core, pcol), device_id_type=MESH,
            ).start()
            return carry

        to_chips(send)
        sent.append((ring_in.at[h, pl.ds(1, chips - 1), nodes], gather_send.at[h, level]))

    def share(level, h):
        nodes = nodes_of(level)
        wait_bytes(ring_in.at[h, pl.ds(1, chips - 1), nodes], gather_recv.at[h, level])
        here = xs.at[h, nodes, pl.ds(own_half, BLOCK_ROWS)]
        pltpu.make_async_remote_copy(
            src_ref=here, dst_ref=here,
            send_sem=share_send.at[h, level], recv_sem=share_recv.at[h, level],
            device_id=(other, pcol), device_id_type=MESH,
        ).start()
        sent.append((pair_in.at[h, nodes], share_send.at[h, level]))

    def multiply(level, h):
        wait_bytes(pair_in.at[h, nodes_of(level)], share_recv.at[h, level])
        for node in each(level):
            x_high, x_low = split(xs[h, node])
            product = dot3(panel_high[node], panel_low[node], x_high, x_low)
            for slot in range(8):
                prod[h, node, slot] = product[slot * BLOCK_ROWS:(slot + 1) * BLOCK_ROWS]

    def store(level, h):
        copy = pltpu.make_async_copy(
            xs.at[h, nodes_of(level)], sol_hbm.at[nodes_of(level), :, pl.ds(h * width, width)],
            out_sem.at[h, level],
        )
        copy.start()
        return copy

    def split_panel(node):
        loads["panel", node].wait()

        def one(step, carry):
            part = pl.ds(step * BLOCK_ROWS, BLOCK_ROWS)
            panel_high[node, part], panel_low[node, part] = split(panel[node, part])
            return carry

        lax.fori_loop(0, 8, one, 0)

    def picked(h, node, block):
        slot = 8
        for i in range(8):
            slot = jnp.where(rows_ref[node, i] == block, i, slot)
        return prod[h, node, slot]

    size = 2 * BLOCK_ROWS // cols
    windows = (pl.ds(0, 2), pl.ds(2, 1))
    targets = (((4, (0, 1)), (5, (2, 3))), ((6, (0, 1, 2, 3, 4, 5)),))

    def send_window(level, h):
        which = windows[level]
        for target, children in targets[level]:
            for b in range(2):
                block = target * super_blocks + prow * 2 + b
                total = picked(h, children[0], block)
                for node in children[1:]:
                    total = total + picked(h, node, block)
                win[h, target - 4, pl.ds(b * BLOCK_ROWS, BLOCK_ROWS)] = total

        def send(i, carry):
            peer = col_peer(i)
            pltpu.make_async_remote_copy(
                src_ref=win.at[h, which, pl.ds(peer * size, size)], dst_ref=win_in.at[h, i, which],
                send_sem=win_send.at[h, level], recv_sem=win_recv.at[h, level],
                device_id=(prow, peer), device_id_type=MESH,
            ).start()
            return carry

        to_cols(send)
        sent.append((win_in.at[h, pl.ds(1, cols - 1), which], win_send.at[h, level]))

    def spread(level, h):
        which = windows[level]
        loads["rhs", h, level + 1].wait()
        wait_bytes(win_in.at[h, pl.ds(1, cols - 1), which], win_recv.at[h, level])
        mine = pl.ds(pcol * size, size)
        for target, _ in targets[level]:
            total = win[h, target - 4, mine]
            for i in range(1, cols):
                total = total + win_in[h, i, target - 4]
            res[h, target - 4, mine] = rhs[h, target, mine] - total
        here = res.at[h, which, mine]

        def send(i, carry):
            pltpu.make_async_remote_copy(
                src_ref=here, dst_ref=here,
                send_sem=back_send.at[h, level], recv_sem=back_recv.at[h, level],
                device_id=(prow, col_peer(i)), device_id_type=MESH,
            ).start()
            return carry

        to_cols(send)
        sent.append((win_in.at[h, pl.ds(1, cols - 1), which], back_send.at[h, level]))

    def begin_next(level, h):
        wait_bytes(win_in.at[h, pl.ds(1, cols - 1), windows[level - 1]], back_recv.at[h, level - 1])
        halves = [split(res[h, node - 4]) for node in each(level)]
        for start in (other_half, own_half):
            part = pl.ds(pl.multiple_of(start, BLOCK_ROWS), BLOCK_ROWS)
            for node, (r_high, r_low) in zip(each(level), halves):
                terms[h, node, part] = dot3(
                    diag_high[node, part], diag_low[node, part], r_high, r_low
                )
            if start is other_half:
                pair(level, h)

    def add_upper(which, h, nodes, fresh):
        count = upper.shape[4] // BLOCK_ROWS

        def one(j, carry):
            block = SUPERNODES * super_blocks + prow * 16 + j
            total = picked(h, nodes[0], block)
            for node in nodes[1:]:
                total = total + picked(h, node, block)
            place = j // count
            part = pl.ds((j % count) * BLOCK_ROWS, BLOCK_ROWS)
            spot = (which, h, place // side, place % side, part)
            upper[spot] = total if fresh else upper[spot] + total
            return carry

        lax.fori_loop(0, cols * count, one, 0)

    up_rows = upper.shape[4] // 2
    row_half = (pl.ds(0, up_rows), pl.ds(up_rows, up_rows))

    def send_upper(which, h):
        for i in range(1, side):
            peer_x, peer_y = lax.rem(col_x + i, side), lax.rem(col_y + i, side)
            pltpu.make_async_remote_copy(
                src_ref=upper.at[which, h, peer_x, :, row_half[0]], dst_ref=up_in.at[which, h, 0, i],
                send_sem=up_send.at[which, h, 0], recv_sem=up_recv.at[which, h, 0],
                device_id=(prow, peer_x * side + col_y), device_id_type=MESH,
            ).start()
            pltpu.make_async_remote_copy(
                src_ref=upper.at[which, h, :, peer_y, row_half[1]], dst_ref=up_in.at[which, h, 1, i],
                send_sem=up_send.at[which, h, 1], recv_sem=up_recv.at[which, h, 1],
                device_id=(prow, col_x * side + peer_y), device_id_type=MESH,
            ).start()
        for way in range(2):
            sent.append((up_in.at[which, h, way, pl.ds(1, side - 1)], up_send.at[which, h, way]))

    def middle_upper(which, h):
        for way in range(2):
            wait_bytes(up_in.at[which, h, way, pl.ds(1, side - 1)], up_recv.at[which, h, way])

            def one(j, carry):
                if way == 0:
                    total = upper[which, h, col_x, j, row_half[0]]
                else:
                    total = upper[which, h, j, col_y, row_half[1]]
                for i in range(1, side):
                    total = total + up_in[which, h, way, i, j]
                up_mid[which, h, way, j] = total
                return carry

            lax.fori_loop(0, side, one, 0)
            for i in range(1, side):
                if way == 0:
                    place = lax.rem(col_y + i, side)
                    peer = col_x * side + place
                else:
                    place = lax.rem(col_x + i, side)
                    peer = place * side + col_y
                pltpu.make_async_remote_copy(
                    src_ref=up_mid.at[which, h, way, place], dst_ref=up_last.at[which, h, way, i],
                    send_sem=last_send.at[which, h, way], recv_sem=last_recv.at[which, h, way],
                    device_id=(prow, peer), device_id_type=MESH,
                ).start()
            sent.append((up_last.at[which, h, way, pl.ds(1, side - 1)], last_send.at[which, h, way]))

    def finish_upper(which, h, fresh):
        for way in range(2):
            wait_bytes(up_last.at[which, h, way, pl.ds(1, side - 1)], last_recv.at[which, h, way])
            total = up_mid[which, h, way, col_y if way == 0 else col_x]
            for i in range(1, side):
                total = total + up_last[which, h, way, i]
            goal = (row_half[way], pl.ds(h * width, width))
            up_out[goal] = total if fresh else up_out[goal] + total

    def drain(count):
        for ref, sem in sent[:count]:
            wait_bytes(ref, sem)
        del sent[:count]

    def run():
        stores = []
        for h in range(2):
            loads["rhs", h, 0].wait()
            if h == 0:
                for node in range(4):
                    split_diag(node)
            begin(0, h)
        pl.semaphore_wait(barrier, chips + cols - 1)
        for h in range(2):
            pair(0, h)
        yield
        for h in range(2):
            scatter(0, h)
        for h in range(2):
            for node in range(SUPERNODES):
                prod[h, node, 8] = jnp.zeros((BLOCK_ROWS, width), F32)
        for node in range(SUPERNODES):
            split_panel(node)
        for node in range(4, SUPERNODES):
            split_diag(node)
        yield
        for h in range(2):
            gather(0, h)
        yield
        for h in range(2):
            share(0, h)
            multiply(0, h)
            send_window(0, h)
        yield
        for h in range(2):
            spread(0, h)
        yield
        for h in range(2):
            stores.append(store(0, h))
            add_upper(0, h, (0, 1, 2, 3), True)
        for h in range(2):
            begin_next(1, h)
        yield
        for h in range(2):
            scatter(1, h)
        for h in range(2):
            send_upper(0, h)
        for h in range(2):
            gather(1, h)
        yield
        share(1, 0)
        multiply(1, 0)
        share(1, 1)
        send_window(1, 0)
        multiply(1, 1)
        send_window(1, 1)
        yield
        for h in range(2):
            stores.append(store(1, h))
            add_upper(1, h, (4, 5), True)
        for h in range(2):
            spread(1, h)
        yield
        for h in range(2):
            begin_next(2, h)
        for h in range(2):
            scatter(2, h)
        for h in range(2):
            middle_upper(0, h)
        for h in range(2):
            gather(2, h)
        yield
        for h in range(2):
            share(2, h)
        early = len(sent)
        for h in range(2):
            multiply(2, h)
            add_upper(1, h, (6,), False)
            send_upper(1, h)
        yield
        for h in range(2):
            stores.append(store(2, h))
            finish_upper(0, h, True)
        drain(early)
        for copy in stores:
            copy.wait()
        for h in range(2):
            middle_upper(1, h)
        for h in range(2):
            finish_upper(1, h, False)
        last = pltpu.make_async_copy(up_out, up_hbm, out_sem.at[0, 3])
        last.start()
        drain(len(sent))
        last.wait()

    for _ in run():
        pass


def copy_out(sol_ref, up_ref, sol_out, up_out, sems):
    copies = [
        pltpu.make_async_copy(sol_ref.at[k], sol_out.at[k], sems.at[k]) for k in range(SUPERNODES)
    ]
    copies.append(pltpu.make_async_copy(up_ref, up_out, sems.at[SUPERNODES]))
    for copy in copies:
        copy.start()
    for copy in copies:
        copy.wait()


def per_device(chips, side, super_blocks, right_side, inverse_diag, panels, block_rows):
    rhs_cols = right_side.shape[2]
    order = right_side.shape[1]
    upper_own = 2 * block_rows.shape[1]
    rows = BLOCK_ROWS // chips
    cols = side * side
    own_upper = upper_own * BLOCK_ROWS // cols
    dma = pltpu.SemaphoreType.DMA
    width = rhs_cols // 2
    scratch = [
        pltpu.VMEM((2, 7, order, width), F32),
        pltpu.VMEM((7, order, order), F32),
        pltpu.VMEM((7, order, order), BF16),
        pltpu.VMEM((7, order, order), BF16),
        pltpu.VMEM(panels.shape, F32),
        pltpu.VMEM(panels.shape, BF16),
        pltpu.VMEM(panels.shape, BF16),
        pltpu.VMEM((2, 7, order, width), F32),
        pltpu.VMEM((2, 7, BLOCK_ROWS, width), F32),
        pltpu.VMEM((2, 7, BLOCK_ROWS, width), F32),
        pltpu.VMEM((2, chips, 7, rows, width), F32),
        pltpu.VMEM((2, 7, order, width), F32),
        pltpu.VMEM((2, 7, 9, BLOCK_ROWS, width), F32),
        pltpu.VMEM((2, 3, order, width), F32),
        pltpu.VMEM((2, cols, 3, order // cols, width), F32),
        pltpu.VMEM((2, 3, order, width), F32),
        pltpu.VMEM((2, 2, side, side, own_upper, width), F32),
        pltpu.VMEM((2, 2, 2, side, side, own_upper // 2, width), F32),
        pltpu.VMEM((2, 2, 2, side, own_upper // 2, width), F32),
        pltpu.VMEM((2, 2, 2, side, own_upper // 2, width), F32),
        pltpu.VMEM((own_upper, rhs_cols), F32),
        dma((2, 3)), dma((7,)), dma((7,)), dma((2, 3)), dma((2, 3)), dma((2, 3)), dma((2, 3)),
        dma((2, 3)), dma((2, 3)), dma((2, 3)), dma((2, 3)), dma((2, 2)), dma((2, 2)), dma((2, 2)), dma((2, 2)),
        dma((2, 2, 2)), dma((2, 2, 2)), dma((2, 2, 2)), dma((2, 2, 2)), dma((2, 4)),
    ]
    anywhere = pl.BlockSpec(memory_space=pl.ANY)
    stay = pl.BlockSpec(memory_space=pltpu.HBM)
    shapes = (
        jax.ShapeDtypeStruct((7, order, rhs_cols), F32),
        jax.ShapeDtypeStruct((own_upper, rhs_cols), F32),
    )
    results = pl.pallas_call(
        functools.partial(kernel, chips, side, super_blocks),
        out_shape=shapes,
        in_specs=[pl.BlockSpec(memory_space=pltpu.SMEM), stay, stay, stay],
        out_specs=(anywhere, anywhere),
        scratch_shapes=scratch,
        compiler_params=pltpu.CompilerParams(
            collective_id=0, has_side_effects=True, vmem_limit_bytes=52 * 1024 * 1024
        ),
    )(block_rows, right_side, inverse_diag, panels)
    return pl.pallas_call(
        copy_out,
        out_shape=shapes,
        in_specs=[pl.BlockSpec(memory_space=pltpu.VMEM)] * 2,
        out_specs=(stay, stay),
        scratch_shapes=[dma((8,))],
        compiler_params=pltpu.CompilerParams(vmem_limit_bytes=8 * 1024 * 1024),
    )(*results)


def solution(mesh):
    chips, side = mesh.shape["prow"] // 2, math.isqrt(mesh.shape["pcol"])
    super_blocks = 2 * mesh.shape["prow"]
    in_specs = (
        P(None, "prow", None),
        P(None, "pcol", "prow"),
        P(None, "prow", "pcol"),
        P(None, "prow"),
    )
    out_specs = (P(None, "pcol", None), P(("prow", "pcol"), None))
    return jax.shard_map(
        functools.partial(per_device, chips, side, super_blocks),
        mesh=mesh, in_specs=in_specs, out_specs=out_specs, check_vma=False,
    )
```
